256 devices in a mesh: energy: 32 (over y, x, core), slab: 8 (over z).
Axes of the slice: x: 4, y: 4, z: 8, core: 2. Of those that a mesh axis runs over, the one named last changes fastest.
Arguments:
- potential_old: float32 [128, 128, 128], P('slab', 'energy'), may hold values from -6 to 6
- charge: float32 [128, 128, 128], P('slab', 'energy'), may hold values from -6 to 6
- permittivity: float32 [128, 128, 128], P('slab', 'energy'), may hold values from 1 to 12
- owner_cell: int32 [32, 256], P('slab'), may hold values from 0 to 65535
- green_free: float32 [32, 32, 2, 256, 256], P('energy', 'slab')
- coupling: float32 [32, 2, 256, 256], P('slab'), may hold values from -0.25 to 0.25
- shifts: int32 [4], replicated, may hold values from 1 to 2, as said below
- occupation: float32 [4], replicated, may hold values from 0.1 to 3
- mode_tiles: float32 [4, 256, 256], replicated, may hold values from -6 to 6
Outputs:
- potential_new: float32 [128, 128, 128], P('slab', 'energy')
- self_energy: float32 [32, 32, 2, 256, 256], P('energy', 'slab')
The draws below stay inside these ranges and needn't reach their ends.
Inputs may be any that keep to these rules, and one draw needn't show every extreme that they name: `shifts`: every whole number from 1 to 2 is the shift of some mode.
All inputs are finite; a program needn't handle non-finite values.
Results may differ from the reference program's by a relative error of at most 0.00023.
Values sent between devices are 32-bit elements; how exact they have to be, the bound alone decides.
A program may use at most 128 MiB of HBM per device.

```python
import math
import jax
import jax.numpy as jnp
from jax import lax

ORBITALS = 256
SLABS = 32
ENERGIES = 32
SLAB_CELLS = 4
CROSS = 128
DEPTH = 128
MODES = 4
SHIFT_MOST = 2


def draw_green_free(key, part):
    array_shape = (ENERGIES, SLABS, 2, ORBITALS, ORBITALS)
    jitter = jax.random.normal(key, array_shape, jnp.float32)
    identity_block = jnp.eye(ORBITALS, dtype=jnp.float32)
    diagonal = jnp.stack([0.75 * identity_block, -0.25 * identity_block])
    return diagonal + jitter * (0.3 / math.sqrt(ORBITALS))


def draw_shifts(key, part):
    leading = jax.random.permutation(jax.random.fold_in(key, 11), SHIFT_MOST).astype(jnp.int32) + 1
    trailing = jax.random.randint(jax.random.fold_in(key, 12), (MODES - SHIFT_MOST,), 1, SHIFT_MOST + 1).astype(jnp.int32)
    return jnp.concatenate([leading, trailing]).astype(jnp.int32)


def with_ends(array, key, low, top_value):
    spot = [jax.random.randint(jax.random.fold_in(key, axis), (), 0, length) for axis, length in enumerate(array.shape)]
    widest = array.shape.index(max(array.shape))
    next_to = spot[:widest] + [(spot[widest] + 1) % array.shape[widest]] + spot[widest + 1:]
    return array.at[tuple(spot)].set(low).at[tuple(next_to)].set(top_value)


def steps_of(own_key, extent, cuts, smallest, largest):
    def one(dim, blocks):
        steps = jax.random.uniform(jax.random.fold_in(jax.random.fold_in(own_key, 6), dim), (blocks,), jnp.float32, smallest / len(cuts), largest / len(cuts))
        return jnp.repeat(jnp.exp(steps), extent[dim] // blocks).reshape((-1,) + (1,) * (len(extent) - dim - 1))

    loudness = one(*cuts[0])
    for cut in cuts[1:]:
        loudness = loudness * one(*cut)
    return loudness


def gaussian(own_key, shape, width, reach, split=(), kind=jnp.bfloat16):
    array = jax.random.normal(own_key, shape, jnp.float32) * width
    if len(split) > 0:
        array = steps_of(own_key, shape, split, -0.22, 0.18) * array
    return jnp.clip(array, min=-reach, max=reach).astype(kind)


def setup_inputs(seed: int = 0) -> dict:
    streams_of = jax.random.split(jax.random.key(seed), 10)
    return {
        "potential_old": gaussian(streams_of[0], (SLABS * SLAB_CELLS, CROSS, DEPTH), 1.0, 6.0, ((0, 8), (1, 32)), jnp.float32),
        "charge": gaussian(streams_of[1], (SLABS * SLAB_CELLS, CROSS, DEPTH), 1.0, 6.0, ((0, 8), (1, 32)), jnp.float32),
        "permittivity": jnp.clip(jnp.exp(math.log(12.0) - 2.4849066 * jax.random.uniform(streams_of[2], (SLABS * SLAB_CELLS, CROSS, DEPTH), jnp.float32) ** steps_of(streams_of[2], (SLABS * SLAB_CELLS, CROSS, DEPTH), ((0, 8), (1, 32)), -0.2, 0.2)), 1.0, 12.0),
        "owner_cell": with_ends(jax.random.randint(streams_of[3], (SLABS, ORBITALS), 0, SLAB_CELLS * CROSS * DEPTH), jax.random.fold_in(streams_of[3], 1), 0, (SLAB_CELLS * CROSS * DEPTH) - 1).astype(jnp.int32),
        "green_free": draw_green_free(jax.random.fold_in(streams_of[9], 71), 0),
        "coupling": gaussian(streams_of[5], (SLABS, 2, ORBITALS, ORBITALS), (7 * ORBITALS // 4) ** -0.5, 0.25, ((0, 8),), jnp.float32),
        "shifts": draw_shifts(jax.random.fold_in(streams_of[9], 71), 0),
        "occupation": jnp.clip(jnp.exp(jax.random.uniform(streams_of[7], (MODES,), jnp.float32, math.log(0.1), math.log(3.0))), 0.1, 3.0),
        "mode_tiles": gaussian(streams_of[8], (MODES, ORBITALS, ORBITALS), 1.0, 6.0, (), jnp.float32),
    }


FULL_PRECISION = lax.Precision.HIGHEST


def complex_product(former, latter):
    real_part = jnp.matmul(former[..., 0, :, :], latter[..., 0, :, :], precision=FULL_PRECISION) - jnp.matmul(former[..., 1, :, :], latter[..., 1, :, :], precision=FULL_PRECISION)
    imag_part = jnp.matmul(former[..., 0, :, :], latter[..., 1, :, :], precision=FULL_PRECISION) + jnp.matmul(former[..., 1, :, :], latter[..., 0, :, :], precision=FULL_PRECISION)
    return jnp.stack([real_part, imag_part], axis=-3)


def flipped(matrix):
    return jnp.swapaxes(matrix, -1, -2)


def neighbour_windows():
    inner = slice(1, -1)
    return [(slice(2, None), inner, inner), (slice(None, -2), inner, inner),
            (inner, slice(2, None), inner), (inner, slice(None, -2), inner),
            (inner, inner, slice(2, None)), (inner, inner, slice(None, -2))]


def relaxed(padded_field, padded_perm, charge):
    centre = padded_perm[1:-1, 1:-1, 1:-1]
    numerator = charge
    denominator = jnp.zeros_like(charge)
    for window_cut in neighbour_windows():
        face_perm = 0.5 * (centre + padded_perm[window_cut])
        numerator = numerator + face_perm * padded_field[window_cut]
        denominator = denominator + face_perm
    return numerator / denominator


def reference(potential_old, charge, permittivity, owner_cell, green_free, coupling, shifts, occupation, mode_tiles):
    potential_new = relaxed(jnp.pad(potential_old, 1), jnp.pad(permittivity, 1), charge)
    flattened = potential_new.reshape(SLABS, SLAB_CELLS * CROSS * DEPTH)
    orbital_potential = jnp.take_along_axis(flattened, owner_cell.astype(jnp.int32), axis=1)

    def one_energy(free_blocks):
        linkage = complex_product(free_blocks, coupling)
        scaled = free_blocks * orbital_potential[:, None, None, :]
        source = free_blocks + complex_product(scaled, free_blocks)

        def advance(running, members):
            link_now, source_now = members
            updated = complex_product(complex_product(link_now, running), flipped(link_now)) + source_now
            return updated, updated

        start = jnp.zeros((2, ORBITALS, ORBITALS), jnp.float32)
        finished, chained = lax.scan(advance, start, (linkage, source))
        return chained

    greens = lax.map(one_energy, green_free)
    margin_zeros = jnp.zeros((SHIFT_MOST,) + greens.shape[1:], jnp.float32)
    padded_greens = jnp.concatenate([margin_zeros, greens, margin_zeros], axis=0)
    self_energy = jnp.zeros_like(greens)
    for member in range(MODES):
        offset = shifts[member].astype(jnp.int32)
        raised = lax.dynamic_slice_in_dim(padded_greens, (SHIFT_MOST + offset).astype(jnp.int32), ENERGIES, 0)
        lowered = lax.dynamic_slice_in_dim(padded_greens, (SHIFT_MOST - offset).astype(jnp.int32), ENERGIES, 0)
        mixed = occupation[member] * raised + (occupation[member] + 1.0) * lowered
        self_energy = self_energy + mode_tiles[member][None, None, None, :, :] * mixed
    return potential_new, self_energy
```

```python
import functools
import math

import jax
import jax.numpy as jnp
from jax import lax
from jax.experimental import pallas as pl
from jax.experimental.pallas import tpu as pltpu
from jax.sharding import PartitionSpec as P

F32 = jnp.float32
BF16 = jnp.bfloat16
MESH = pl.DeviceIdType.MESH
K_PIECES = 4


def split(x):
    high = x.astype(BF16)
    return high, (x - high.astype(F32)).astype(BF16)


def cprod(left, right, transposed=False):
    (ah, al), (bh, bl) = left, right
    n = ah.shape[-1]
    ah, al = ah.reshape(2 * n, n), al.reshape(2 * n, n)
    dims = (((1,), (1 if transposed else 0,)), ((), ()))

    def real(part):
        dot = functools.partial(lax.dot_general, dimension_numbers=dims, preferred_element_type=F32)
        return dot(ah, bh[part]) + dot(al, bh[part]) + dot(ah, bl[part])

    u, w = real(0), real(1)
    return u[:n] - w[n:], u[n:] + w[:n]


def pair_split(parts):
    (rh, rl), (ih, il) = split(parts[0]), split(parts[1])
    return (rh, ih), (rl, il)


def sandwich(link, state):
    inner = cprod(split(state), link, transposed=True)
    return cprod(link, pair_split(inner))


def kernel(
    ne,
    nz,
    pot,
    charge,
    perm,
    owner,
    g_hbm,
    cpl_hbm,
    shifts,
    occ,
    tiles_hbm,
    pot_out,
    se_hbm,
    g,
    cpl,
    tiles,
    hs_lo,
    hs_hi,
    zs_lo,
    zs_hi,
    hr_before,
    hr_after,
    zr_before,
    zr_after,
    pad_f,
    pad_p,
    cells,
    ar_loc,
    ar_mid,
    ar_row,
    ar_col,
    orb,
    g_nb,
    link_h,
    link_l,
    src,
    p_own,
    s_own,
    p_even,
    s_even,
    q_h,
    q_l,
    k_in,
    k_out,
    carry,
    carry_nb,
    greens,
    greens_nb,
    sib_own,
    sib_nb,
    weight,
    se,
    send_sem,
    recv_sem,
    local_sem,
):
    n0, n1, n2 = pot.shape
    slabs, n = owner.shape
    slab_cells = n0 // slabs
    row = min(8, ne)
    cols = ne // row
    e, z = lax.axis_index("energy"), lax.axis_index("slab")
    core = lax.rem(e, 2)
    sibling = (e + 1 - 2 * core, z)
    odd = lax.rem(z, 2) == 1

    def energy(by):
        return (lax.rem(e + (by + ne), ne), z)

    def level(by):
        return (e, lax.rem(z + (by + nz), nz))

    def in_row(k):
        base = (e // row) * row
        return (base + lax.rem(e - base + k, row), z)

    def remote(source, target, index, device):
        return pltpu.make_async_remote_copy(
            src_ref=source,
            dst_ref=target,
            send_sem=send_sem.at[index],
            recv_sem=recv_sem.at[index],
            device_id=device,
            device_id_type=MESH,
        )

    HALO, ROW, COL, GEX = 0, 4, 11, 14
    PAIR = GEX + 2 * slabs
    KUP, KDOWN = PAIR + 2, PAIR + 2 + K_PIECES
    CARRY = KDOWN + K_PIECES
    SIB = CARRY + 2
    SIBN = SIB + slabs

    load_g = pltpu.make_async_copy(g_hbm.at[0], g, local_sem.at[0])
    load_c = pltpu.make_async_copy(cpl_hbm, cpl, local_sem.at[1])
    load_t = pltpu.make_async_copy(tiles_hbm, tiles, local_sem.at[2])
    load_g.start()
    load_c.start()
    load_t.start()

    partners = [in_row(k) for k in range(1, row)] + [energy(row * k) for k in range(1, cols)]
    partners += [energy(by) for by in (1, -1, 2, -2)] + [level(by) for by in (1, -1, 2, -2)]
    barrier = pltpu.get_barrier_semaphore()
    for device in partners:
        pl.semaphore_signal(barrier, inc=1, device_id=device, device_id_type=MESH)

    for index, ref in enumerate((pot, perm)):
        hs_lo[index] = ref[:, 0:1, :]
        hs_hi[index] = ref[:, n1 - 1 : n1, :]
        zs_lo[index] = ref[0]
        zs_hi[index] = ref[n0 - 1]
    pl.semaphore_wait(barrier, len(partners))

    halos = [
        remote(hs_lo, hr_after, HALO, energy(-1)),
        remote(hs_hi, hr_before, HALO + 1, energy(1)),
        remote(zs_lo, zr_after, HALO + 2, level(-1)),
        remote(zs_hi, zr_before, HALO + 3, level(1)),
    ]
    for copy in halos:
        copy.start()

    load_g.wait()
    load_c.wait()

    def make_link(which, s, block):
        made = cprod(split(block), split(cpl[s]))
        for part in range(2):
            link_h[which, s, part], link_l[which, s, part] = split(made[part])

    def make_source(which, s, block):
        scaled = block * orb[pl.ds(s, 1), :]
        made = cprod(split(scaled), split(block))
        for part in range(2):
            src[which, s, part] = block[part] + made[part]

    @pl.loop(0, slabs)
    def _(s):
        make_link(2, s, g[s])

    for copy in halos:
        copy.wait()
    for index, (ref, pad) in enumerate(((pot, pad_f), (perm, pad_p))):
        pad[1 : n0 + 1, 1 : n1 + 1, :] = ref[...]
        pad[1 : n0 + 1, 0:1, :] = jnp.where(e > 0, hr_before[index], 0.0)
        pad[1 : n0 + 1, n1 + 1 : n1 + 2, :] = jnp.where(e < ne - 1, hr_after[index], 0.0)
        pad[0, 1 : n1 + 1, :] = jnp.where(z > 0, zr_before[index], 0.0)
        pad[n0 + 1, 1 : n1 + 1, :] = jnp.where(z < nz - 1, zr_after[index], 0.0)
    centre = perm[...]
    field = pot[...]
    lane = lax.broadcasted_iota(jnp.int32, (n0, n1, n2), 2)
    inner0, inner1 = slice(1, n0 + 1), slice(1, n1 + 1)
    windows = [
        (pad_f[2 : n0 + 2, inner1, :], pad_p[2 : n0 + 2, inner1, :]),
        (pad_f[0:n0, inner1, :], pad_p[0:n0, inner1, :]),
        (pad_f[inner0, 2 : n1 + 2, :], pad_p[inner0, 2 : n1 + 2, :]),
        (pad_f[inner0, 0:n1, :], pad_p[inner0, 0:n1, :]),
    ]
    for shift, edge in ((n2 - 1, n2 - 1), (1, 0)):
        windows.append(
            tuple(jnp.where(lane == edge, 0.0, pltpu.roll(x, shift, 2)) for x in (field, centre))
        )
    numerator = charge[...]
    denominator = jnp.zeros_like(numerator)
    for near_field, near_perm in windows:
        face = 0.5 * (centre + near_perm)
        numerator = numerator + face * near_field
        denominator = denominator + face
    swept = numerator / denominator
    pot_out[...] = swept
    for plane in range(n0):
        cells[pl.ds(plane * n1, n1), :] = swept[plane]

    depth_bits = int(math.log2(n2))
    cross_bits = int(math.log2(n1 * ne))
    rows = slab_cells * n1
    for s in range(slabs):
        index = owner[s : s + 1, :]
        first = index >> (depth_bits + cross_bits)
        second = ((index >> depth_bits) & (n1 * ne - 1)) - e * n1
        third = index & (n2 - 1)
        chosen = jnp.where(
            lax.broadcasted_iota(jnp.int32, (n2, n), 0) == third, 1.0, 0.0
        ).astype(BF16)
        block = cells[pl.ds(s * rows, rows), :]
        high, low = split(block)
        lowest = (block - high.astype(F32) - low.astype(F32)).astype(BF16)
        picked = sum(
            jnp.dot(piece, chosen, preferred_element_type=F32) for piece in (high, low, lowest)
        )
        here = (second >= 0) & (second < n1)
        at = jnp.where(here, first * n1 + second, -1)
        mine = lax.broadcasted_iota(jnp.int32, (rows, n), 0) == at
        ar_loc[s : s + 1, :] = jnp.sum(jnp.where(mine, picked, 0.0), axis=0, keepdims=True)

    row_copies = [remote(ar_loc, ar_row.at[k - 1], ROW + k - 1, in_row(k)) for k in range(1, row)]
    for copy in row_copies:
        copy.start()

    for part in range(2):
        p_own[part] = link_h[2, 0, part].astype(F32) + link_l[2, 0, part].astype(F32)

    @pl.loop(1, slabs)
    def _(s):
        made = cprod((link_h[2, s], link_l[2, s]), split(p_own[...]))
        for part in range(2):
            p_own[part] = made[part]

    send_p = remote(p_own, p_even, PAIR, level(1))

    @pl.when(jnp.logical_not(odd))
    def _():
        send_p.start()

    for copy in row_copies:
        copy.wait()
    total = ar_loc[...]
    for k in range(1, row):
        total = total + ar_row[k - 1]
    ar_mid[...] = total
    col_copies = [
        remote(ar_mid, ar_col.at[k - 1], COL + k - 1, energy(row * k)) for k in range(1, cols)
    ]
    for copy in col_copies:
        copy.start()
    for copy in col_copies:
        copy.wait()
    total = ar_mid[...]
    for k in range(1, cols):
        total = total + ar_col[k - 1]
    orb[...] = total

    def g_copy(s, to_upper):
        side = 0 if to_upper else 1
        return remote(
            g.at[s], g_nb.at[side, s], GEX + side * slabs + s, energy(2 if to_upper else -2)
        )

    for s in range(slabs):
        g_copy(s, True).start()
        g_copy(s, False).start()

    @pl.loop(0, slabs)
    def _(s):
        make_source(2, s, g[s])

    s_own[...] = src[2, 0]

    @pl.loop(1, slabs)
    def _(s):
        made = sandwich((link_h[2, s], link_l[2, s]), s_own[...])
        for part in range(2):
            s_own[part] = made[part] + src[2, s, part]

    send_s = remote(s_own, s_even, PAIR + 1, level(1))

    @pl.when(jnp.logical_not(odd))
    def _():
        send_s.start()

    def make_weights():
        load_t.wait()
        for offset in (1, 2):
            raise_now = jnp.zeros((n, n), F32)
            lower_now = jnp.zeros((n, n), F32)
            for mode in range(tiles.shape[0]):
                hit = jnp.where(shifts[mode] == offset, 1.0, 0.0)
                raise_now = raise_now + (hit * occ[mode]) * tiles[mode]
                lower_now = lower_now + (hit * (occ[mode] + 1.0)) * tiles[mode]
            raise_now = jnp.where(e + offset < ne, raise_now, 0.0)
            lower_now = jnp.where(e >= offset, lower_now, 0.0)
            if offset == 2:
                weight[0], weight[1] = lower_now, raise_now
            else:
                weight[2] = jnp.where(core == 0, raise_now, lower_now)
                weight[3] = jnp.where(core == 0, lower_now, raise_now)

    def prepare_neighbours():
        @pl.loop(0, slabs)
        def _(s):
            for side in range(2):
                g_copy(s, side == 0).wait_recv()
                block = g_nb[side, s]
                make_link(side, s, block)
                make_source(side, s, block)

    early = jnp.logical_or(jnp.logical_not(odd), z == nz - 1)

    make_weights()

    def k_slices():
        half = n // (K_PIECES // 2)
        return [(part, pl.ds(h * half, half)) for part in range(2) for h in range(K_PIECES // 2)]

    def k_up(i):
        at = k_slices()[i]
        return remote(k_out.at[at], k_in.at[at], KUP + i, level(2))

    def k_down(i):
        at = k_slices()[i]
        return remote(k_in.at[at], k_in.at[at], KDOWN + i, level(-1))

    @pl.when(odd)
    def _():
        send_p.wait_recv()
        made = cprod((split(p_own[...])), split(p_even[...]))
        for part in range(2):
            q_h[part], q_l[part] = split(made[part])
        send_s.wait_recv()
        made = sandwich(split(p_own[...]), s_even[...])
        for part in range(2):
            s_own[part] = made[part] + s_own[part]

    @pl.when(early)
    def _():
        prepare_neighbours()

    @pl.when(z == 1)
    def _():
        k_out[...] = s_own[...]
        carry[...] = s_even[...]

    @pl.when(jnp.logical_and(odd, z > 1))
    def _():
        for i in range(K_PIECES):
            k_up(i).wait_recv()
            k_down(i).start()

        @pl.when(z < nz - 1)
        def _():
            made = sandwich((q_h[...], q_l[...]), k_in[...])
            for part in range(2):
                k_out[part] = made[part] + s_own[part]

    @pl.when(jnp.logical_and(odd, z < nz - 1))
    def _():
        for i in range(K_PIECES):
            k_up(i).start()

    @pl.when(jnp.logical_and(odd, z > 1))
    def _():
        made = sandwich(split(p_even[...]), k_in[...])
        for part in range(2):
            carry[part] = made[part] + s_even[part]

    @pl.when(z == 0)
    def _():
        carry[...] = jnp.zeros_like(carry)

    @pl.when(jnp.logical_and(jnp.logical_not(odd), z > 0))
    def _():
        for i in range(K_PIECES):
            k_down(i).wait_recv()
        carry[...] = k_in[...]

    def carry_copy(side):
        return remote(carry, carry_nb.at[side], CARRY + side, energy(2 if side == 0 else -2))

    for side in range(2):
        carry_copy(side).start()

    def own_copy(s):
        return remote(greens.at[s], sib_own.at[s], SIB + s, sibling)

    for s in range(slabs):
        pass

    def own_green(s, before):
        made = sandwich((link_h[2, s], link_l[2, s]), before)
        for part in range(2):
            greens[s, part] = made[part] + src[2, s, part]
        own_copy(s).start()

    own_green(0, carry[...])

    @pl.loop(1, slabs)
    def _(s):
        own_green(s, greens[s - 1])

    @pl.when(jnp.logical_not(early))
    def _():
        prepare_neighbours()

    def carry_arrived(side):
        pltpu.make_async_remote_copy(
            src_ref=carry,
            dst_ref=carry_nb.at[side],
            send_sem=send_sem.at[CARRY + side],
            recv_sem=recv_sem.at[CARRY + side],
            device_id=sibling,
            device_id_type=MESH,
        ).wait_recv()

    def far_copy(side, s):
        return remote(greens_nb.at[side, s], sib_nb.at[s], SIBN + s, sibling)

    def far_green(side, s):
        @pl.when(s == 0)
        def _():
            carry_arrived(side)
            k_in[...] = carry_nb[side]

        made = sandwich((link_h[side, s], link_l[side, s]), k_in[...])
        for part in range(2):
            value = made[part] + src[side, s, part]
            greens_nb[side, s, part] = value
            k_in[part] = value

    @pl.when(jnp.logical_and(odd, z > 1))
    def _():
        for i in range(K_PIECES):
            k_down(i).wait_send()

    @pl.loop(0, slabs)
    def _(s):
        far_green(1 - core, s)
        far_copy(1 - core, s).start()

    def se_copy(s):
        return pltpu.make_async_copy(se.at[s], se_hbm.at[0, s], local_sem.at[3 + s])

    @pl.loop(0, slabs)
    def _(s):
        far_green(core, s)
        own_copy(s).wait_recv()
        far_copy(0, s).wait_recv()
        for part in range(2):
            se[s, part] = (
                weight[0] * greens_nb[0, s, part]
                + weight[1] * greens_nb[1, s, part]
                + weight[2] * sib_own[s, part]
                + weight[3] * sib_nb[s, part]
            )
        se_copy(s).start()

    for s in range(slabs):
        g_copy(s, True).wait_send()
        g_copy(s, False).wait_send()
        own_copy(s).wait_send()
        far_copy(0, s).wait_send()
        se_copy(s).wait()
    for side in range(2):
        carry_copy(side).wait_send()

    @pl.when(jnp.logical_not(odd))
    def _():
        send_p.wait_send()
        send_s.wait_send()

    @pl.when(jnp.logical_and(odd, z < nz - 1))
    def _():
        for i in range(K_PIECES):
            k_up(i).wait_send()


def per_device(
    ne,
    nz,
    potential_old,
    charge,
    permittivity,
    owner_cell,
    green_free,
    coupling,
    shifts,
    occupation,
    mode_tiles,
):
    n0, n1, n2 = potential_old.shape
    slabs, n = owner_cell.shape
    modes = mode_tiles.shape[0]
    vmem = pl.BlockSpec(memory_space=pltpu.VMEM)
    smem = pl.BlockSpec(memory_space=pltpu.SMEM)
    hbm = pl.BlockSpec(memory_space=pl.ANY)
    row = min(8, ne)
    cols = ne // row
    block = (2, n, n)
    sems = 14 + 2 * slabs + 2 + 2 * K_PIECES + 2 + 2 * slabs
    scratch = [
        pltpu.VMEM((slabs,) + block, F32),
        pltpu.VMEM((slabs,) + block, F32),
        pltpu.VMEM((modes, n, n), F32),
        pltpu.VMEM((2, n0, 1, n2), F32),
        pltpu.VMEM((2, n0, 1, n2), F32),
        pltpu.VMEM((2, n1, n2), F32),
        pltpu.VMEM((2, n1, n2), F32),
        pltpu.VMEM((2, n0, 1, n2), F32),
        pltpu.VMEM((2, n0, 1, n2), F32),
        pltpu.VMEM((2, n1, n2), F32),
        pltpu.VMEM((2, n1, n2), F32),
        pltpu.VMEM((n0 + 2, 8, n2), F32),
        pltpu.VMEM((n0 + 2, 8, n2), F32),
        pltpu.VMEM((n0 * n1, n2), F32),
        pltpu.VMEM((slabs, n), F32),
        pltpu.VMEM((slabs, n), F32),
        pltpu.VMEM((row, slabs, n), F32),
        pltpu.VMEM((cols, slabs, n), F32),
        pltpu.VMEM((slabs, n), F32),
        pltpu.VMEM((2, slabs) + block, F32),
        pltpu.VMEM((3, slabs) + block, BF16),
        pltpu.VMEM((3, slabs) + block, BF16),
        pltpu.VMEM((3, slabs) + block, F32),
        pltpu.VMEM(block, F32),
        pltpu.VMEM(block, F32),
        pltpu.VMEM(block, F32),
        pltpu.VMEM(block, F32),
        pltpu.VMEM(block, BF16),
        pltpu.VMEM(block, BF16),
        pltpu.VMEM(block, F32),
        pltpu.VMEM(block, F32),
        pltpu.VMEM(block, F32),
        pltpu.VMEM((2,) + block, F32),
        pltpu.VMEM((slabs,) + block, F32),
        pltpu.VMEM((2, slabs) + block, F32),
        pltpu.VMEM((slabs,) + block, F32),
        pltpu.VMEM((slabs,) + block, F32),
        pltpu.VMEM((4, n, n), F32),
        pltpu.VMEM((slabs,) + block, F32),
        pltpu.SemaphoreType.DMA((sems,)),
        pltpu.SemaphoreType.DMA((sems,)),
        pltpu.SemaphoreType.DMA((3 + slabs,)),
    ]
    return pl.pallas_call(
        functools.partial(kernel, ne, nz),
        out_shape=(
            jax.ShapeDtypeStruct((n0, n1, n2), F32),
            jax.ShapeDtypeStruct((1, slabs) + block, F32),
        ),
        in_specs=[vmem, vmem, vmem, vmem, hbm, hbm, smem, smem, hbm],
        out_specs=(vmem, hbm),
        scratch_shapes=scratch,
        compiler_params=pltpu.CompilerParams(
            collective_id=0, has_side_effects=True, vmem_limit_bytes=60 << 20
        ),
    )(
        potential_old,
        charge,
        permittivity,
        owner_cell,
        green_free,
        coupling,
        shifts,
        occupation,
        mode_tiles,
    )


def solution(mesh):
    in_specs = (
        P("slab", "energy", None),
        P("slab", "energy", None),
        P("slab", "energy", None),
        P("slab", None),
        P("energy", "slab", None, None, None),
        P("slab", None, None, None),
        P(),
        P(),
        P(),
    )
    out_specs = (P("slab", "energy", None), P("energy", "slab", None, None, None))
    return jax.shard_map(
        functools.partial(per_device, mesh.shape["energy"], mesh.shape["slab"]),
        mesh=mesh,
        in_specs=in_specs,
        out_specs=out_specs,
        check_vma=False,
    )
```

```python
import functools
import math

import jax
import jax.numpy as jnp
from jax import lax
from jax.experimental import pallas as pl
from jax.experimental.pallas import tpu as pltpu
from jax.sharding import PartitionSpec as P

F32 = jnp.float32
BF16 = jnp.bfloat16
MESH = pl.DeviceIdType.MESH
K_PIECES = 4


def split(x):
    high = x.astype(BF16)
    return high, (x - high.astype(F32)).astype(BF16)


def split3(real, imag):
    return split(real), split(imag), split(real + imag)


def cprod(left, right, transposed=False):
    dims = (((1,), (1 if transposed else 0,)), ((), ()))
    dot = functools.partial(lax.dot_general, dimension_numbers=dims, preferred_element_type=F32)
    first, second, third = (
        dot(a[0], b[0]) + dot(a[1], b[0]) + dot(a[0], b[1]) for a, b in zip(left, right)
    )
    return first - second, third - first - second


def kernel(
    ne,
    nz,
    pot,
    charge,
    perm,
    owner,
    g_hbm,
    cpl_hbm,
    shifts,
    occ,
    tiles_hbm,
    pot_out,
    se_hbm,
    g,
    cpl,
    tiles,
    hs_lo,
    hs_hi,
    zs_lo,
    zs_hi,
    hr_before,
    hr_after,
    zr_before,
    zr_after,
    pad_f,
    pad_p,
    cells,
    ar_loc,
    ar_mid,
    ar_row,
    ar_col,
    orb,
    g_nb,
    link_h,
    link_l,
    src,
    p_own,
    s_own,
    p_even,
    s_even,
    map_h,
    map_l,
    tmp,
    k_in,
    k_out,
    carry,
    carry_nb,
    greens,
    greens_nb,
    sib_own,
    sib_nb,
    weight,
    se,
    send_sem,
    recv_sem,
    local_sem,
):
    n0, n1, n2 = pot.shape
    slabs, n = owner.shape
    slab_cells = n0 // slabs
    row = min(8, ne)
    cols = ne // row
    e, z = lax.axis_index("energy"), lax.axis_index("slab")
    core = lax.rem(e, 2)
    sibling = (e + 1 - 2 * core, z)
    odd = lax.rem(z, 2) == 1

    def energy(by):
        return (lax.rem(e + (by + ne), ne), z)

    def level(by):
        return (e, lax.rem(z + (by + nz), nz))

    def in_row(k):
        base = (e // row) * row
        return (base + lax.rem(e - base + k, row), z)

    def remote(source, target, index, device):
        return pltpu.make_async_remote_copy(
            src_ref=source,
            dst_ref=target,
            send_sem=send_sem.at[index],
            recv_sem=recv_sem.at[index],
            device_id=device,
            device_id_type=MESH,
        )

    HALO, ROW, COL, GEX = 0, 4, 11, 14
    PAIR = GEX + 2 * slabs
    KUP, KDOWN = PAIR + 2, PAIR + 2 + K_PIECES
    CARRY = KDOWN + K_PIECES
    SIB = CARRY + 2
    SIBN = SIB + slabs

    load_g = pltpu.make_async_copy(g_hbm.at[0], g, local_sem.at[0])
    load_c = pltpu.make_async_copy(cpl_hbm, cpl, local_sem.at[1])
    load_t = pltpu.make_async_copy(tiles_hbm, tiles, local_sem.at[2])
    load_g.start()
    load_c.start()
    load_t.start()

    partners = [in_row(k) for k in range(1, row)] + [energy(row * k) for k in range(1, cols)]
    partners += [energy(by) for by in (1, -1, 2, -2)] + [level(by) for by in (1, -1, 2, -2)]
    barrier = pltpu.get_barrier_semaphore()
    for device in partners:
        pl.semaphore_signal(barrier, inc=1, device_id=device, device_id_type=MESH)

    for index, ref in enumerate((pot, perm)):
        hs_lo[index] = ref[:, 0:1, :]
        hs_hi[index] = ref[:, n1 - 1 : n1, :]
        zs_lo[index] = ref[0]
        zs_hi[index] = ref[n0 - 1]
    pl.semaphore_wait(barrier, len(partners))

    halos = [
        remote(hs_lo, hr_after, HALO, energy(-1)),
        remote(hs_hi, hr_before, HALO + 1, energy(1)),
        remote(zs_lo, zr_after, HALO + 2, level(-1)),
        remote(zs_hi, zr_before, HALO + 3, level(1)),
    ]
    for copy in halos:
        copy.start()

    load_g.wait()

    def g_copy(s, to_upper):
        side = 0 if to_upper else 1
        return remote(
            g.at[s], g_nb.at[side, s], GEX + side * slabs + s, energy(2 if to_upper else -2)
        )

    for s in range(slabs):
        g_copy(s, True).start()
        g_copy(s, False).start()

    load_c.wait()
    EVEN, ODD, BOTH, HALF = range(4)

    def keep(high, low, at, parts):
        for k, (h, l) in enumerate(split3(*parts)):
            high[(*at, k)], low[(*at, k)] = h, l

    def link(which, s):
        return [(link_h[which, s, k], link_l[which, s, k]) for k in range(3)]

    def mapping(which):
        return [(map_h[which, k], map_l[which, k]) for k in range(3)]

    def three(ref, *at):
        return split3(ref[(*at, 0)], ref[(*at, 1)])

    def sandwiches(*jobs):
        for slot, (outer, state, _) in enumerate(jobs):
            tmp[slot, 0], tmp[slot, 1] = cprod(state(), outer(), transposed=True)
        for slot, (outer, _, write) in enumerate(jobs):
            write(*cprod(outer(), three(tmp, slot)))

    def added(target, at, *terms):
        def write(real, imag):
            for part, value in enumerate((real, imag)):
                target[(*at, part)] = value + sum(ref[(*where, part)] for ref, where in terms)

        return write

    def make_links(s, *pairs):
        factor = three(cpl, s)
        for which, ref, at in pairs:
            keep(link_h, link_l, (which, s), cprod(three(ref, *at), factor))

    def make_sources(s, *pairs):
        scale = orb[pl.ds(s, 1), :]
        for which, ref, at in pairs:
            real, imag = ref[(*at, 0)], ref[(*at, 1)]
            made = cprod(split3(real * scale, imag * scale), split3(real, imag))
            src[which, s, 0], src[which, s, 1] = real + made[0], imag + made[1]

    @pl.loop(0, slabs)
    def _(s):
        make_links(s, (2, g, (s,)))

    for copy in halos:
        copy.wait()
    for index, (ref, pad) in enumerate(((pot, pad_f), (perm, pad_p))):
        pad[1 : n0 + 1, 1 : n1 + 1, :] = ref[...]
        pad[1 : n0 + 1, 0:1, :] = jnp.where(e > 0, hr_before[index], 0.0)
        pad[1 : n0 + 1, n1 + 1 : n1 + 2, :] = jnp.where(e < ne - 1, hr_after[index], 0.0)
        pad[0, 1 : n1 + 1, :] = jnp.where(z > 0, zr_before[index], 0.0)
        pad[n0 + 1, 1 : n1 + 1, :] = jnp.where(z < nz - 1, zr_after[index], 0.0)
    centre = perm[...]
    field = pot[...]
    lane = lax.broadcasted_iota(jnp.int32, (n0, n1, n2), 2)
    inner0, inner1 = slice(1, n0 + 1), slice(1, n1 + 1)
    windows = [
        (pad_f[2 : n0 + 2, inner1, :], pad_p[2 : n0 + 2, inner1, :]),
        (pad_f[0:n0, inner1, :], pad_p[0:n0, inner1, :]),
        (pad_f[inner0, 2 : n1 + 2, :], pad_p[inner0, 2 : n1 + 2, :]),
        (pad_f[inner0, 0:n1, :], pad_p[inner0, 0:n1, :]),
    ]
    for shift, edge in ((n2 - 1, n2 - 1), (1, 0)):
        windows.append(
            tuple(jnp.where(lane == edge, 0.0, pltpu.roll(x, shift, 2)) for x in (field, centre))
        )
    numerator = charge[...]
    denominator = jnp.zeros_like(numerator)
    for near_field, near_perm in windows:
        face = 0.5 * (centre + near_perm)
        numerator = numerator + face * near_field
        denominator = denominator + face
    swept = numerator / denominator
    pot_out[...] = swept
    for plane in range(n0):
        cells[pl.ds(plane * n1, n1), :] = swept[plane]

    depth_bits = int(math.log2(n2))
    cross_bits = int(math.log2(n1 * ne))
    rows = slab_cells * n1
    for s in range(slabs):
        index = owner[s : s + 1, :]
        first = index >> (depth_bits + cross_bits)
        second = ((index >> depth_bits) & (n1 * ne - 1)) - e * n1
        third = index & (n2 - 1)
        chosen = jnp.where(
            lax.broadcasted_iota(jnp.int32, (n2, n), 0) == third, 1.0, 0.0
        ).astype(BF16)
        block = cells[pl.ds(s * rows, rows), :]
        high, low = split(block)
        lowest = (block - high.astype(F32) - low.astype(F32)).astype(BF16)
        picked = sum(
            jnp.dot(piece, chosen, preferred_element_type=F32) for piece in (high, low, lowest)
        )
        here = (second >= 0) & (second < n1)
        at = jnp.where(here, first * n1 + second, -1)
        mine = lax.broadcasted_iota(jnp.int32, (rows, n), 0) == at
        ar_loc[s : s + 1, :] = jnp.sum(jnp.where(mine, picked, 0.0), axis=0, keepdims=True)

    row_copies = [remote(ar_loc, ar_row.at[k - 1], ROW + k - 1, in_row(k)) for k in range(1, row)]
    for copy in row_copies:
        copy.start()

    tmp[0, 0], tmp[0, 1] = cprod(link(2, 1), link(2, 0))
    keep(map_h, map_l, (HALF,), cprod(link(2, 3), link(2, 2)))
    p_own[0], p_own[1] = cprod(mapping(HALF), three(tmp, 0))

    send_p = remote(p_own, p_even, PAIR, level(1))

    @pl.when(jnp.logical_not(odd))
    def _():
        send_p.start()

    for copy in row_copies:
        copy.wait()
    total = ar_loc[...]
    for k in range(1, row):
        total = total + ar_row[k - 1]
    ar_mid[...] = total
    col_copies = [
        remote(ar_mid, ar_col.at[k - 1], COL + k - 1, energy(row * k)) for k in range(1, cols)
    ]
    for copy in col_copies:
        copy.start()
    for copy in col_copies:
        copy.wait()
    total = ar_mid[...]
    for k in range(1, cols):
        total = total + ar_col[k - 1]
    orb[...] = total

    @pl.loop(0, slabs)
    def _(s):
        make_sources(s, (2, g, (s,)))

    sandwiches(
        (lambda: link(2, 1), lambda: three(src, 2, 0), added(carry, (), (src, (2, 1)))),
        (lambda: link(2, 3), lambda: three(src, 2, 2), added(k_out, (), (src, (2, 3)))),
    )
    sandwiches((lambda: mapping(HALF), lambda: three(carry), added(s_own, (), (k_out, ()))))

    send_s = remote(s_own, s_even, PAIR + 1, level(1))

    @pl.when(jnp.logical_not(odd))
    def _():
        send_s.start()

    def make_weights():
        load_t.wait()
        for offset in (1, 2):
            raise_now = jnp.zeros((n, n), F32)
            lower_now = jnp.zeros((n, n), F32)
            for mode in range(tiles.shape[0]):
                hit = jnp.where(shifts[mode] == offset, 1.0, 0.0)
                raise_now = raise_now + (hit * occ[mode]) * tiles[mode]
                lower_now = lower_now + (hit * (occ[mode] + 1.0)) * tiles[mode]
            raise_now = jnp.where(e + offset < ne, raise_now, 0.0)
            lower_now = jnp.where(e >= offset, lower_now, 0.0)
            if offset == 2:
                weight[0], weight[1] = lower_now, raise_now
            else:
                weight[2] = jnp.where(core == 0, raise_now, lower_now)
                weight[3] = jnp.where(core == 0, lower_now, raise_now)

    def prepare_neighbours():
        @pl.loop(0, slabs)
        def _(s):
            for side in range(2):
                g_copy(s, side == 0).wait_recv()
            both = [(side, g_nb, (side, s)) for side in range(2)]
            make_links(s, *both)
            make_sources(s, *both)

    early = jnp.logical_or(jnp.logical_not(odd), z == nz - 1)

    make_weights()

    def k_slices():
        half = n // (K_PIECES // 2)
        return [(part, pl.ds(h * half, half)) for part in range(2) for h in range(K_PIECES // 2)]

    def k_up(i):
        at = k_slices()[i]
        return remote(k_out.at[at], k_in.at[at], KUP + i, level(2))

    def k_down(i):
        at = k_slices()[i]
        return remote(k_in.at[at], k_in.at[at], KDOWN + i, level(-1))

    @pl.when(odd)
    def _():
        send_p.wait_recv()
        keep(map_h, map_l, (ODD,), (p_own[0], p_own[1]))
        keep(map_h, map_l, (EVEN,), (p_even[0], p_even[1]))
        keep(map_h, map_l, (BOTH,), cprod(mapping(ODD), mapping(EVEN)))
        send_s.wait_recv()
        sandwiches((lambda: mapping(ODD), lambda: three(s_even), added(s_own, (), (s_own, ()))))

    @pl.when(early)
    def _():
        prepare_neighbours()

    @pl.when(z == 1)
    def _():
        k_out[...] = s_own[...]
        carry[...] = s_even[...]

    @pl.when(jnp.logical_and(odd, z > 1))
    def _():
        for i in range(K_PIECES):
            k_up(i).wait_recv()
            k_down(i).start()

        @pl.when(z < nz - 1)
        def _():
            sandwiches((lambda: mapping(BOTH), lambda: three(k_in), added(k_out, (), (s_own, ()))))

    @pl.when(jnp.logical_and(odd, z < nz - 1))
    def _():
        for i in range(K_PIECES):
            k_up(i).start()

    @pl.when(jnp.logical_and(odd, z > 1))
    def _():
        sandwiches((lambda: mapping(EVEN), lambda: three(k_in), added(carry, (), (s_even, ()))))

    @pl.when(z == 0)
    def _():
        carry[...] = jnp.zeros_like(carry)

    @pl.when(jnp.logical_and(jnp.logical_not(odd), z > 0))
    def _():
        for i in range(K_PIECES):
            k_down(i).wait_recv()
        carry[...] = k_in[...]

    def carry_copy(side):
        return remote(carry, carry_nb.at[side], CARRY + side, energy(2 if side == 0 else -2))

    for side in range(2):
        carry_copy(side).start()

    def own_copy(s):
        return remote(greens.at[s], sib_own.at[s], SIB + s, sibling)

    def own_green(s, ref, at):
        sandwiches(
            (lambda: link(2, s), lambda: three(ref, *at), added(greens, (s,), (src, (2, s))))
        )
        own_copy(s).start()

    own_green(0, carry, ())

    @pl.loop(1, slabs)
    def _(s):
        own_green(s, greens, (s - 1,))

    @pl.when(jnp.logical_not(early))
    def _():
        prepare_neighbours()

    def carry_arrived(side):
        pltpu.make_async_remote_copy(
            src_ref=carry,
            dst_ref=carry_nb.at[side],
            send_sem=send_sem.at[CARRY + side],
            recv_sem=recv_sem.at[CARRY + side],
            device_id=sibling,
            device_id_type=MESH,
        ).wait_recv()

    def far_copy(side, s):
        return remote(greens_nb.at[side, s], sib_nb.at[s], SIBN + s, sibling)

    def far_greens(s, ref, at):
        sandwiches(
            *(
                (
                    lambda side=side: link(side, s),
                    lambda side=side: three(ref, side, *at),
                    added(greens_nb, (side, s), (src, (side, s))),
                )
                for side in range(2)
            )
        )
        far_copy(1 - core, s).start()

    def se_copy(s):
        return pltpu.make_async_copy(se.at[s], se_hbm.at[0, s], local_sem.at[3 + s])

    def mix(s):
        own_copy(s).wait_recv()
        far_copy(0, s).wait_recv()
        for part in range(2):
            se[s, part] = (
                weight[0] * greens_nb[0, s, part]
                + weight[1] * greens_nb[1, s, part]
                + weight[2] * sib_own[s, part]
                + weight[3] * sib_nb[s, part]
            )
        se_copy(s).start()

    for side in range(2):
        carry_arrived(side)
    far_greens(0, carry_nb, ())

    @pl.loop(1, slabs)
    def _(s):
        far_greens(s, greens_nb, (s - 1,))
        mix(s - 1)

    mix(slabs - 1)

    for s in range(slabs):
        g_copy(s, True).wait_send()
        g_copy(s, False).wait_send()
        own_copy(s).wait_send()
        far_copy(0, s).wait_send()
        se_copy(s).wait()
    for side in range(2):
        carry_copy(side).wait_send()

    @pl.when(jnp.logical_not(odd))
    def _():
        send_p.wait_send()
        send_s.wait_send()

    @pl.when(jnp.logical_and(odd, z < nz - 1))
    def _():
        for i in range(K_PIECES):
            k_up(i).wait_send()

    @pl.when(jnp.logical_and(odd, z > 1))
    def _():
        for i in range(K_PIECES):
            k_down(i).wait_send()


def per_device(
    ne,
    nz,
    potential_old,
    charge,
    permittivity,
    owner_cell,
    green_free,
    coupling,
    shifts,
    occupation,
    mode_tiles,
):
    n0, n1, n2 = potential_old.shape
    slabs, n = owner_cell.shape
    modes = mode_tiles.shape[0]
    vmem = pl.BlockSpec(memory_space=pltpu.VMEM)
    smem = pl.BlockSpec(memory_space=pltpu.SMEM)
    hbm = pl.BlockSpec(memory_space=pl.ANY)
    row = min(8, ne)
    cols = ne // row
    block = (2, n, n)
    sems = 14 + 2 * slabs + 2 + 2 * K_PIECES + 2 + 2 * slabs
    scratch = [
        pltpu.VMEM((slabs,) + block, F32),
        pltpu.VMEM((slabs,) + block, F32),
        pltpu.VMEM((modes, n, n), F32),
        pltpu.VMEM((2, n0, 1, n2), F32),
        pltpu.VMEM((2, n0, 1, n2), F32),
        pltpu.VMEM((2, n1, n2), F32),
        pltpu.VMEM((2, n1, n2), F32),
        pltpu.VMEM((2, n0, 1, n2), F32),
        pltpu.VMEM((2, n0, 1, n2), F32),
        pltpu.VMEM((2, n1, n2), F32),
        pltpu.VMEM((2, n1, n2), F32),
        pltpu.VMEM((n0 + 2, 8, n2), F32),
        pltpu.VMEM((n0 + 2, 8, n2), F32),
        pltpu.VMEM((n0 * n1, n2), F32),
        pltpu.VMEM((slabs, n), F32),
        pltpu.VMEM((slabs, n), F32),
        pltpu.VMEM((row, slabs, n), F32),
        pltpu.VMEM((cols, slabs, n), F32),
        pltpu.VMEM((slabs, n), F32),
        pltpu.VMEM((2, slabs) + block, F32),
        pltpu.VMEM((3, slabs, 3, n, n), BF16),
        pltpu.VMEM((3, slabs, 3, n, n), BF16),
        pltpu.VMEM((3, slabs) + block, F32),
        pltpu.VMEM(block, F32),
        pltpu.VMEM(block, F32),
        pltpu.VMEM(block, F32),
        pltpu.VMEM(block, F32),
        pltpu.VMEM((4, 3, n, n), BF16),
        pltpu.VMEM((4, 3, n, n), BF16),
        pltpu.VMEM((2,) + block, F32),
        pltpu.VMEM(block, F32),
        pltpu.VMEM(block, F32),
        pltpu.VMEM(block, F32),
        pltpu.VMEM((2,) + block, F32),
        pltpu.VMEM((slabs,) + block, F32),
        pltpu.VMEM((2, slabs) + block, F32),
        pltpu.VMEM((slabs,) + block, F32),
        pltpu.VMEM((slabs,) + block, F32),
        pltpu.VMEM((4, n, n), F32),
        pltpu.VMEM((slabs,) + block, F32),
        pltpu.SemaphoreType.DMA((sems,)),
        pltpu.SemaphoreType.DMA((sems,)),
        pltpu.SemaphoreType.DMA((3 + slabs,)),
    ]
    return pl.pallas_call(
        functools.partial(kernel, ne, nz),
        out_shape=(
            jax.ShapeDtypeStruct((n0, n1, n2), F32),
            jax.ShapeDtypeStruct((1, slabs) + block, F32),
        ),
        in_specs=[vmem, vmem, vmem, vmem, hbm, hbm, smem, smem, hbm],
        out_specs=(vmem, hbm),
        scratch_shapes=scratch,
        compiler_params=pltpu.CompilerParams(
            collective_id=0, has_side_effects=True, vmem_limit_bytes=60 << 20
        ),
    )(
        potential_old,
        charge,
        permittivity,
        owner_cell,
        green_free,
        coupling,
        shifts,
        occupation,
        mode_tiles,
    )


def solution(mesh):
    in_specs = (
        P("slab", "energy", None),
        P("slab", "energy", None),
        P("slab", "energy", None),
        P("slab", None),
        P("energy", "slab", None, None, None),
        P("slab", None, None, None),
        P(),
        P(),
        P(),
    )
    out_specs = (P("slab", "energy", None), P("energy", "slab", None, None, None))
    return jax.shard_map(
        functools.partial(per_device, mesh.shape["energy"], mesh.shape["slab"]),
        mesh=mesh,
        in_specs=in_specs,
        out_specs=out_specs,
        check_vma=False,
    )
```

```python
import functools
import math

import jax
import jax.numpy as jnp
from jax import lax
from jax.experimental import pallas as pl
from jax.experimental.pallas import tpu as pltpu
from jax.sharding import PartitionSpec as P

F32 = jnp.float32
BF16 = jnp.bfloat16
MESH = pl.DeviceIdType.MESH
K_PIECES = 8


def split(x):
    high = x.astype(BF16)
    return high, (x - high.astype(F32)).astype(BF16)


def split3(real, imag):
    return split(real), split(imag), split(real + imag)


def cprod(left, right, transposed=False):
    dims = (((1,), (1 if transposed else 0,)), ((), ()))
    dot = functools.partial(lax.dot_general, dimension_numbers=dims, preferred_element_type=F32)
    first, second, third = (
        dot(a[0], b[0]) + dot(a[1], b[0]) + dot(a[0], b[1]) for a, b in zip(left, right)
    )
    return first - second, third - first - second


def kernel(
    ne,
    nz,
    pot,
    charge,
    perm,
    owner,
    g_hbm,
    cpl_hbm,
    shifts,
    occ,
    tiles_hbm,
    pot_out,
    se_hbm,
    g,
    cpl,
    tiles,
    hs_lo,
    hs_hi,
    zs_lo,
    zs_hi,
    hr_before,
    hr_after,
    zr_before,
    zr_after,
    pad_f,
    pad_p,
    cells,
    ar_loc,
    ar_mid,
    ar_row,
    ar_col,
    orb,
    g_nb,
    link_h,
    link_l,
    src,
    p_own,
    s_own,
    p_even,
    s_even,
    map_h,
    map_l,
    tmp,
    map_in,
    state_in,
    k_in,
    k_out,
    carry,
    greens,
    greens_nb,
    sib_own,
    sib_nb,
    weight,
    se,
    send_sem,
    recv_sem,
    local_sem,
):
    n0, n1, n2 = pot.shape
    slabs, n = owner.shape
    slab_cells = n0 // slabs
    assert (nz, slabs) == (8, 4)
    row = min(8, ne)
    cols = ne // row
    e, z = lax.axis_index("energy"), lax.axis_index("slab")
    core = lax.rem(e, 2)
    sibling = (e + 1 - 2 * core, z)
    odd = lax.rem(z, 2) == 1

    def energy(by):
        return (lax.rem(e + (by + ne), ne), z)

    def level(by):
        return (e, lax.rem(z + (by + nz), nz))

    def in_row(k):
        base = (e // row) * row
        return (base + lax.rem(e - base + k, row), z)

    def remote(source, target, index, device):
        return pltpu.make_async_remote_copy(
            src_ref=source,
            dst_ref=target,
            send_sem=send_sem.at[index],
            recv_sem=recv_sem.at[index],
            device_id=device,
            device_id_type=MESH,
        )

    HALO, ROW, COL, GEX = 0, 4, 11, 14
    PAIR = GEX + 2 * slabs
    KUP, KDOWN, KBACK = (PAIR + 2 + i * K_PIECES for i in range(3))
    KSIDE = KUP
    AHEAD = KBACK + K_PIECES
    CARRY = AHEAD + 2
    SIB = CARRY + 2
    SIBN = SIB + slabs

    load_g = pltpu.make_async_copy(g_hbm.at[0], g, local_sem.at[0])
    load_c = pltpu.make_async_copy(cpl_hbm, cpl, local_sem.at[1])
    load_t = pltpu.make_async_copy(tiles_hbm, tiles, local_sem.at[2])
    load_g.start()
    load_c.start()
    load_t.start()

    partners = [in_row(k) for k in range(1, row)] + [energy(row * k) for k in range(1, cols)]
    partners += [energy(by) for by in (1, -1, 2, -2)] + [level(by) for by in (1, -1, 2, -2)]
    barrier = pltpu.get_barrier_semaphore()
    for device in partners:
        pl.semaphore_signal(barrier, inc=1, device_id=device, device_id_type=MESH)

    for index, ref in enumerate((pot, perm)):
        hs_lo[index] = ref[:, 0:1, :]
        hs_hi[index] = ref[:, n1 - 1 : n1, :]
        zs_lo[index] = ref[0]
        zs_hi[index] = ref[n0 - 1]
    pl.semaphore_wait(barrier, len(partners))

    halos = [
        remote(hs_lo, hr_after, HALO, energy(-1)),
        remote(hs_hi, hr_before, HALO + 1, energy(1)),
        remote(zs_lo, zr_after, HALO + 2, level(-1)),
        remote(zs_hi, zr_before, HALO + 3, level(1)),
    ]
    for copy in halos:
        copy.start()

    load_g.wait()

    def g_copy(s, to_upper):
        side = 0 if to_upper else 1
        return remote(
            g.at[s], g_nb.at[side, s], GEX + side * slabs + s, energy(2 if to_upper else -2)
        )

    load_c.wait()
    EVEN, ODD, BOTH, HALF = range(4)

    def keep(high, low, at, parts):
        for k, (h, l) in enumerate(split3(*parts)):
            high[(*at, k)], low[(*at, k)] = h, l

    def link(which, s):
        return [(link_h[which, s, k], link_l[which, s, k]) for k in range(3)]

    def mapping(which):
        return [(map_h[which, k], map_l[which, k]) for k in range(3)]

    def three(ref, *at):
        return split3(ref[(*at, 0)], ref[(*at, 1)])

    def sandwiches(*jobs):
        for slot, (outer, state, _) in enumerate(jobs):
            tmp[slot, 0], tmp[slot, 1] = cprod(state(), outer(), transposed=True)
        for slot, (outer, _, write) in enumerate(jobs):
            write(*cprod(outer(), three(tmp, slot)))

    def added(target, at, *terms):
        def write(real, imag):
            for part, value in enumerate((real, imag)):
                target[(*at, part)] = value + sum(ref[(*where, part)] for ref, where in terms)

        return write

    def make_links(s, *pairs):
        factor = three(cpl, s)
        for which, ref, at in pairs:
            keep(link_h, link_l, (which, s), cprod(three(ref, *at), factor))

    def make_sources(s, *pairs):
        scale = orb[pl.ds(s, 1), :]
        for which, ref, at in pairs:
            real, imag = ref[(*at, 0)], ref[(*at, 1)]
            made = cprod(split3(real * scale, imag * scale), split3(real, imag))
            src[which, s, 0], src[which, s, 1] = real + made[0], imag + made[1]

    @pl.loop(0, slabs)
    def _(s):
        make_links(s, (2, g, (s,)))

    for copy in halos:
        copy.wait()
    for index, (ref, pad) in enumerate(((pot, pad_f), (perm, pad_p))):
        pad[1 : n0 + 1, 1 : n1 + 1, :] = ref[...]
        pad[1 : n0 + 1, 0:1, :] = jnp.where(e > 0, hr_before[index], 0.0)
        pad[1 : n0 + 1, n1 + 1 : n1 + 2, :] = jnp.where(e < ne - 1, hr_after[index], 0.0)
        pad[0, 1 : n1 + 1, :] = jnp.where(z > 0, zr_before[index], 0.0)
        pad[n0 + 1, 1 : n1 + 1, :] = jnp.where(z < nz - 1, zr_after[index], 0.0)
    centre = perm[...]
    field = pot[...]
    lane = lax.broadcasted_iota(jnp.int32, (n0, n1, n2), 2)
    inner0, inner1 = slice(1, n0 + 1), slice(1, n1 + 1)
    windows = [
        (pad_f[2 : n0 + 2, inner1, :], pad_p[2 : n0 + 2, inner1, :]),
        (pad_f[0:n0, inner1, :], pad_p[0:n0, inner1, :]),
        (pad_f[inner0, 2 : n1 + 2, :], pad_p[inner0, 2 : n1 + 2, :]),
        (pad_f[inner0, 0:n1, :], pad_p[inner0, 0:n1, :]),
    ]
    for shift, edge in ((n2 - 1, n2 - 1), (1, 0)):
        windows.append(
            tuple(jnp.where(lane == edge, 0.0, pltpu.roll(x, shift, 2)) for x in (field, centre))
        )
    numerator = charge[...]
    denominator = jnp.zeros_like(numerator)
    for near_field, near_perm in windows:
        face = 0.5 * (centre + near_perm)
        numerator = numerator + face * near_field
        denominator = denominator + face
    swept = numerator / denominator
    pot_out[...] = swept
    for plane in range(n0):
        cells[pl.ds(plane * n1, n1), :] = swept[plane]

    depth_bits = int(math.log2(n2))
    cross_bits = int(math.log2(n1 * ne))
    rows = slab_cells * n1
    for s in range(slabs):
        index = owner[s : s + 1, :]
        first = index >> (depth_bits + cross_bits)
        second = ((index >> depth_bits) & (n1 * ne - 1)) - e * n1
        third = index & (n2 - 1)
        chosen = jnp.where(
            lax.broadcasted_iota(jnp.int32, (n2, n), 0) == third, 1.0, 0.0
        ).astype(BF16)
        block = cells[pl.ds(s * rows, rows), :]
        high, low = split(block)
        lowest = (block - high.astype(F32) - low.astype(F32)).astype(BF16)
        picked = sum(
            jnp.dot(piece, chosen, preferred_element_type=F32) for piece in (high, low, lowest)
        )
        here = (second >= 0) & (second < n1)
        at = jnp.where(here, first * n1 + second, -1)
        mine = lax.broadcasted_iota(jnp.int32, (rows, n), 0) == at
        ar_loc[s : s + 1, :] = jnp.sum(jnp.where(mine, picked, 0.0), axis=0, keepdims=True)

    row_copies = [remote(ar_loc, ar_row.at[k - 1], ROW + k - 1, in_row(k)) for k in range(1, row)]
    for copy in row_copies:
        copy.start()

    tmp[0, 0], tmp[0, 1] = cprod(link(2, 1), link(2, 0))
    keep(map_h, map_l, (HALF,), cprod(link(2, 3), link(2, 2)))
    p_own[0], p_own[1] = cprod(mapping(HALF), three(tmp, 0))

    send_p = remote(p_own, p_even, PAIR, level(1))

    @pl.when(jnp.logical_and(jnp.logical_not(odd), z > 0))
    def _():
        send_p.start()

    for copy in row_copies:
        copy.wait()
    total = ar_loc[...]
    for k in range(1, row):
        total = total + ar_row[k - 1]
    ar_mid[...] = total
    col_copies = [
        remote(ar_mid, ar_col.at[k - 1], COL + k - 1, energy(row * k)) for k in range(1, cols)
    ]
    for copy in col_copies:
        copy.start()
    for copy in col_copies:
        copy.wait()
    total = ar_mid[...]
    for k in range(1, cols):
        total = total + ar_col[k - 1]
    orb[...] = total

    for s in range(1, slabs):
        g_copy(s, True).start()
        g_copy(s, False).start()

    @pl.loop(0, slabs)
    def _(s):
        make_sources(s, (2, g, (s,)))

    sandwiches(
        (lambda: link(2, 1), lambda: three(src, 2, 0), added(carry, (), (src, (2, 1)))),
        (lambda: link(2, 3), lambda: three(src, 2, 2), added(k_out, (), (src, (2, 3)))),
    )
    sandwiches((lambda: mapping(HALF), lambda: three(carry), added(s_own, (), (k_out, ()))))

    send_s = remote(s_own, s_even, PAIR + 1, level(1))

    @pl.when(jnp.logical_not(odd))
    def _():
        send_s.start()

    def make_weights():
        load_t.wait()
        for offset in (1, 2):
            raise_now = jnp.zeros((n, n), F32)
            lower_now = jnp.zeros((n, n), F32)
            for mode in range(tiles.shape[0]):
                hit = jnp.where(shifts[mode] == offset, 1.0, 0.0)
                raise_now = raise_now + (hit * occ[mode]) * tiles[mode]
                lower_now = lower_now + (hit * (occ[mode] + 1.0)) * tiles[mode]
            raise_now = jnp.where(e + offset < ne, raise_now, 0.0)
            lower_now = jnp.where(e >= offset, lower_now, 0.0)
            if offset == 2:
                weight[0], weight[1] = lower_now, raise_now
            else:
                weight[2] = jnp.where(core == 0, raise_now, lower_now)
                weight[3] = jnp.where(core == 0, lower_now, raise_now)

    def prepare_neighbours():
        @pl.loop(1, slabs)
        def _(s):
            for side in range(2):
                g_copy(s, side == 0).wait_recv()
            both = [(side, g_nb, (side, s)) for side in range(2)]
            make_links(s, *both)
            make_sources(s, *both)

    make_weights()

    def k_slices():
        rows_each = n // (K_PIECES // 2)
        return [
            (part, pl.ds(h * rows_each, rows_each))
            for h in range(K_PIECES // 2)
            for part in range(2)
        ]

    def k_piece(source, first, i, device):
        at = k_slices()[i]
        return remote(source.at[at], k_in.at[at], first + i, device)

    pieces = range(K_PIECES)
    k_up = [k_piece(k_out, KUP, i, level(2)) for i in pieces]
    k_down = [k_piece(k_in, KDOWN, i, level(-1)) for i in pieces]
    k_side = [k_piece(k_in, KSIDE, i, level(1)) for i in pieces]
    k_back = [k_piece(k_out, KBACK, i, level(-2)) for i in pieces]
    k_relay = [k_piece(k_in, KBACK, i, level(-2)) for i in pieces]
    ahead = [
        remote(p_even, map_in, AHEAD, level(1)),
        remote(s_own, state_in, AHEAD + 1, level(1)),
    ]
    ahead_relay = [
        remote(map_in, map_in, AHEAD, level(1)),
        remote(state_in, state_in, AHEAD + 1, level(1)),
    ]

    def pair_state():
        keep(map_h, map_l, (ODD,), (p_own[0], p_own[1]))
        send_s.wait_recv()
        sandwiches((lambda: mapping(ODD), lambda: three(s_even), added(s_own, (), (s_own, ()))))

    def pair_maps():
        send_p.wait_recv()
        keep(map_h, map_l, (EVEN,), (p_even[0], p_even[1]))

    def into_carry(which, state):
        sandwiches((lambda: mapping(which), lambda: three(k_in), added(carry, (), (state, ()))))

    def receive_and_hand_on(copies, *onward):
        for i in pieces:
            copies[i].wait_recv()
            for copy in onward:
                copy[i].start()

    early = jnp.logical_or(jnp.logical_not(odd), z > 4)

    @pl.when(z == 0)
    def _():
        carry[...] = jnp.zeros_like(carry)

    @pl.when(z == 1)
    def _():
        pair_state()
        k_out[...] = s_own[...]
        for copy in k_up:
            copy.start()
        carry[...] = s_even[...]

    @pl.when(jnp.logical_or(z == 3, z == 5))
    def _():
        pair_maps()
        keep(map_h, map_l, (ODD,), (p_own[0], p_own[1]))
        both = cprod(mapping(ODD), mapping(EVEN))

        @pl.when(z == 3)
        def _():
            keep(map_h, map_l, (BOTH,), both)

        @pl.when(z == 5)
        def _():
            p_even[0], p_even[1] = both
            ahead[0].start()

        pair_state()

        @pl.when(z == 5)
        def _():
            ahead[1].start()

    @pl.when(z == 7)
    def _():
        pair_maps()
        send_s.wait_recv()
        ahead[0].wait_recv()
        keep(map_h, map_l, (BOTH,), cprod(mapping(EVEN), three(map_in)))

    @pl.when(z == 6)
    def _():
        for copy, relay in zip(ahead, ahead_relay):
            copy.wait_recv()
            relay.start()
        keep(map_h, map_l, (BOTH,), (map_in[0], map_in[1]))

    @pl.when(early)
    def _():
        prepare_neighbours()

    @pl.when(z == 3)
    def _():
        receive_and_hand_on(k_up, k_down)
        sandwiches((lambda: mapping(BOTH), lambda: three(k_in), added(k_out, (), (s_own, ()))))
        for forward, backward in zip(k_up, k_back):
            backward.start()
            forward.start()

    @pl.when(z == 5)
    def _():
        receive_and_hand_on(k_up, k_side, k_down)

    @pl.when(jnp.logical_or(z == 3, z == 5))
    def _():
        into_carry(EVEN, s_even)

    @pl.when(z == 7)
    def _():
        ahead[1].wait_recv()
        sandwiches(
            (lambda: mapping(EVEN), lambda: three(state_in), added(k_out, (), (s_even, ())))
        )
        receive_and_hand_on(k_back)
        into_carry(BOTH, k_out)

    @pl.when(jnp.logical_or(z == 2, z == 4))
    def _():
        receive_and_hand_on(k_down)
        carry[...] = k_in[...]

    @pl.when(z == 6)
    def _():
        receive_and_hand_on(k_side)
        into_carry(BOTH, state_in)

    def first_copy(side):
        return remote(
            greens.at[0],
            greens_nb.at[side, 0],
            CARRY + side,
            energy(2 if side == 0 else -2),
        )

    def own_copy(s):
        return remote(greens.at[s], sib_own.at[s], SIB + s, sibling)

    def own_green(s, ref, at):
        sandwiches(
            (lambda: link(2, s), lambda: three(ref, *at), added(greens, (s,), (src, (2, s))))
        )

    own_green(0, carry, ())
    for side in range(2):
        first_copy(side).start()
    own_copy(0).start()

    @pl.loop(1, slabs)
    def _(s):
        own_green(s, greens, (s - 1,))
        own_copy(s).start()

    @pl.when(z == 1)
    def _():
        receive_and_hand_on(k_back, k_relay)

    @pl.when(jnp.logical_not(early))
    def _():
        prepare_neighbours()

    def far_copy(side, s):
        return remote(greens_nb.at[side, s], sib_nb.at[s], SIBN + s, sibling)

    def far_green(side, s):
        sandwiches(
            (
                lambda: link(side, s),
                lambda: three(greens_nb, side, s - 1),
                added(greens_nb, (side, s), (src, (side, s))),
            )
        )

    def se_copy(s):
        return pltpu.make_async_copy(se.at[s], se_hbm.at[0, s], local_sem.at[3 + s])

    def mix(s):
        own_copy(s).wait_recv()
        far_copy(0, s).wait_recv()
        for part in range(2):
            se[s, part] = (
                weight[0] * greens_nb[0, s, part]
                + weight[1] * greens_nb[1, s, part]
                + weight[2] * sib_own[s, part]
                + weight[3] * sib_nb[s, part]
            )
        se_copy(s).start()

    for side in range(2):
        first_copy(side).wait_recv()
    far_copy(1 - core, 0).start()

    @pl.loop(1, slabs)
    def _(s):
        far_green(1 - core, s)
        far_copy(1 - core, s).start()

    @pl.loop(1, slabs)
    def _(s):
        far_green(core, s)
        mix(s - 1)

    mix(slabs - 1)

    for s in range(slabs):
        own_copy(s).wait_send()
        far_copy(0, s).wait_send()
        se_copy(s).wait()
    for s in range(1, slabs):
        g_copy(s, True).wait_send()
        g_copy(s, False).wait_send()
    for side in range(2):
        first_copy(side).wait_send()

    def sent(condition, *copies):
        @pl.when(condition)
        def _():
            for copy in copies:
                copy.wait_send()

    sent(jnp.logical_not(odd), send_s)
    sent(jnp.logical_and(jnp.logical_not(odd), z > 0), send_p)
    sent(jnp.logical_or(z == 1, z == 3), *k_up)
    sent(jnp.logical_or(z == 3, z == 5), *k_down)
    sent(z == 5, *k_side)
    sent(z == 3, *k_back)
    sent(z == 1, *k_relay)
    sent(z == 5, *ahead)
    sent(z == 6, *ahead_relay)


def per_device(
    ne,
    nz,
    potential_old,
    charge,
    permittivity,
    owner_cell,
    green_free,
    coupling,
    shifts,
    occupation,
    mode_tiles,
):
    n0, n1, n2 = potential_old.shape
    slabs, n = owner_cell.shape
    modes = mode_tiles.shape[0]
    vmem = pl.BlockSpec(memory_space=pltpu.VMEM)
    smem = pl.BlockSpec(memory_space=pltpu.SMEM)
    hbm = pl.BlockSpec(memory_space=pl.ANY)
    row = min(8, ne)
    cols = ne // row
    block = (2, n, n)
    sems = 14 + 2 * slabs + 2 + 3 * K_PIECES + 2 + 2 + 2 * slabs
    scratch = [
        pltpu.VMEM((slabs,) + block, F32),
        pltpu.VMEM((slabs,) + block, F32),
        pltpu.VMEM((modes, n, n), F32),
        pltpu.VMEM((2, n0, 1, n2), F32),
        pltpu.VMEM((2, n0, 1, n2), F32),
        pltpu.VMEM((2, n1, n2), F32),
        pltpu.VMEM((2, n1, n2), F32),
        pltpu.VMEM((2, n0, 1, n2), F32),
        pltpu.VMEM((2, n0, 1, n2), F32),
        pltpu.VMEM((2, n1, n2), F32),
        pltpu.VMEM((2, n1, n2), F32),
        pltpu.VMEM((n0 + 2, 8, n2), F32),
        pltpu.VMEM((n0 + 2, 8, n2), F32),
        pltpu.VMEM((n0 * n1, n2), F32),
        pltpu.VMEM((slabs, n), F32),
        pltpu.VMEM((slabs, n), F32),
        pltpu.VMEM((row, slabs, n), F32),
        pltpu.VMEM((cols, slabs, n), F32),
        pltpu.VMEM((slabs, n), F32),
        pltpu.VMEM((2, slabs) + block, F32),
        pltpu.VMEM((3, slabs, 3, n, n), BF16),
        pltpu.VMEM((3, slabs, 3, n, n), BF16),
        pltpu.VMEM((3, slabs) + block, F32),
        pltpu.VMEM(block, F32),
        pltpu.VMEM(block, F32),
        pltpu.VMEM(block, F32),
        pltpu.VMEM(block, F32),
        pltpu.VMEM((4, 3, n, n), BF16),
        pltpu.VMEM((4, 3, n, n), BF16),
        pltpu.VMEM((2,) + block, F32),
        pltpu.VMEM(block, F32),
        pltpu.VMEM(block, F32),
        pltpu.VMEM(block, F32),
        pltpu.VMEM(block, F32),
        pltpu.VMEM(block, F32),
        pltpu.VMEM((slabs,) + block, F32),
        pltpu.VMEM((2, slabs) + block, F32),
        pltpu.VMEM((slabs,) + block, F32),
        pltpu.VMEM((slabs,) + block, F32),
        pltpu.VMEM((4, n, n), F32),
        pltpu.VMEM((slabs,) + block, F32),
        pltpu.SemaphoreType.DMA((sems,)),
        pltpu.SemaphoreType.DMA((sems,)),
        pltpu.SemaphoreType.DMA((3 + slabs,)),
    ]
    return pl.pallas_call(
        functools.partial(kernel, ne, nz),
        out_shape=(
            jax.ShapeDtypeStruct((n0, n1, n2), F32),
            jax.ShapeDtypeStruct((1, slabs) + block, F32),
        ),
        in_specs=[vmem, vmem, vmem, vmem, hbm, hbm, smem, smem, hbm],
        out_specs=(vmem, hbm),
        scratch_shapes=scratch,
        compiler_params=pltpu.CompilerParams(
            collective_id=0, has_side_effects=True, vmem_limit_bytes=60 << 20
        ),
    )(
        potential_old,
        charge,
        permittivity,
        owner_cell,
        green_free,
        coupling,
        shifts,
        occupation,
        mode_tiles,
    )


def solution(mesh):
    in_specs = (
        P("slab", "energy", None),
        P("slab", "energy", None),
        P("slab", "energy", None),
        P("slab", None),
        P("energy", "slab", None, None, None),
        P("slab", None, None, None),
        P(),
        P(),
        P(),
    )
    out_specs = (P("slab", "energy", None), P("energy", "slab", None, None, None))
    return jax.shard_map(
        functools.partial(per_device, mesh.shape["energy"], mesh.shape["slab"]),
        mesh=mesh,
        in_specs=in_specs,
        out_specs=out_specs,
        check_vma=False,
    )
```

```python
import functools
import math

import jax
import jax.numpy as jnp
from jax import lax
from jax.experimental import pallas as pl
from jax.experimental.pallas import tpu as pltpu
from jax.sharding import PartitionSpec as P

F32 = jnp.float32
BF16 = jnp.bfloat16
MESH = pl.DeviceIdType.MESH
K_PIECES = 8
K_AHEAD = 2


def split(x):
    high = x.astype(BF16)
    return high, (x - high.astype(F32)).astype(BF16)


def split3(real, imag):
    return split(real), split(imag), split(real + imag)


def cprod(left, right, transposed=False):
    dims = (((1,), (1 if transposed else 0,)), ((), ()))
    dot = functools.partial(lax.dot_general, dimension_numbers=dims, preferred_element_type=F32)
    first, second, third = (
        dot(a[0], b[0]) + dot(a[1], b[0]) + dot(a[0], b[1]) for a, b in zip(left, right)
    )
    return first - second, third - first - second


def kernel(
    ne,
    nz,
    pot_hbm,
    charge_hbm,
    perm_hbm,
    owner_hbm,
    g_hbm,
    cpl_hbm,
    shifts,
    occ,
    tiles_hbm,
    pot_out,
    se_out,
    pot,
    charge,
    perm,
    owner,
    g,
    cpl,
    tiles,
    hs_lo,
    hs_hi,
    zs_lo,
    zs_hi,
    hr_before,
    hr_after,
    zr_before,
    zr_after,
    pad_f,
    pad_p,
    cells,
    ar_loc,
    ar_mid,
    ar_row,
    ar_col,
    orb,
    g_nb,
    link_h,
    link_l,
    src,
    p_own,
    s_own,
    p_even,
    s_even,
    map_h,
    map_l,
    tmp,
    map_in,
    state_in,
    k_in,
    k_out,
    base,
    greens,
    greens_nb,
    sib_own,
    sib_nb,
    weight,
    send_sem,
    recv_sem,
    local_sem,
):
    n0, n1, n2 = pot.shape
    slabs, n = owner.shape
    slab_cells = n0 // slabs
    assert (nz, slabs) == (8, 4)
    row = min(8, ne)
    cols = ne // row
    e, z = lax.axis_index("energy"), lax.axis_index("slab")
    core = lax.rem(e, 2)
    sibling = (e + 1 - 2 * core, z)
    odd = lax.rem(z, 2) == 1

    def energy(by):
        return (lax.rem(e + (by + ne), ne), z)

    def level(by):
        return (e, lax.rem(z + (by + nz), nz))

    def in_row(k):
        base = (e // row) * row
        return (base + lax.rem(e - base + k, row), z)

    def remote(source, target, index, device):
        return pltpu.make_async_remote_copy(
            src_ref=source,
            dst_ref=target,
            send_sem=send_sem.at[index],
            recv_sem=recv_sem.at[index],
            device_id=device,
            device_id_type=MESH,
        )

    HALO, ROW = 0, 4
    COL = ROW + row - 1
    GEX = COL + cols - 1
    PAIR = GEX + 2 * slabs
    KUP, KDOWN, KBACK = (PAIR + 2 + i * K_PIECES for i in range(3))
    KSIDE = KUP
    AHEAD = KBACK + K_PIECES
    CARRY = AHEAD + 2
    SIB = CARRY + 2
    SIBN = SIB + slabs

    load_small = [
        pltpu.make_async_copy(source, target, local_sem.at[3 + i])
        for i, (source, target) in enumerate(
            ((pot_hbm, pot), (perm_hbm, perm), (charge_hbm, charge), (owner_hbm, owner))
        )
    ]
    for copy in load_small:
        copy.start()
    load_g = pltpu.make_async_copy(g_hbm.at[0], g, local_sem.at[0])
    load_c = pltpu.make_async_copy(cpl_hbm, cpl, local_sem.at[1])
    load_t = pltpu.make_async_copy(tiles_hbm, tiles, local_sem.at[2])
    partners = [in_row(k) for k in range(1, row)] + [energy(row * k) for k in range(1, cols)]
    partners += [energy(by) for by in (1, -1, 2, -2)] + [level(by) for by in (1, -1, 2, -2)]
    barrier = pltpu.get_barrier_semaphore()
    for device in partners:
        pl.semaphore_signal(barrier, inc=1, device_id=device, device_id_type=MESH)

    load_g.start()
    load_c.start()
    load_t.start()
    load_small[0].wait()
    load_small[1].wait()
    for index, ref in enumerate((pot, perm)):
        hs_lo[index] = ref[:, 0:1, :]
        hs_hi[index] = ref[:, n1 - 1 : n1, :]
        zs_lo[index] = ref[0]
        zs_hi[index] = ref[n0 - 1]
    pl.semaphore_wait(barrier, len(partners))

    halos = [
        remote(hs_lo, hr_after, HALO, energy(-1)),
        remote(hs_hi, hr_before, HALO + 1, energy(1)),
        remote(zs_lo, zr_after, HALO + 2, level(-1)),
        remote(zs_hi, zr_before, HALO + 3, level(1)),
    ]
    for copy in halos:
        copy.start()

    load_g.wait()

    def g_copy(s, to_upper):
        side = 0 if to_upper else 1
        return remote(
            g.at[s], g_nb.at[side, s], GEX + side * slabs + s, energy(2 if to_upper else -2)
        )

    load_c.wait()
    EVEN, ODD, BOTH, HALF, FIRST = range(5)

    def keep(high, low, at, parts):
        for k, (h, l) in enumerate(split3(*parts)):
            high[(*at, k)], low[(*at, k)] = h, l

    def link(which, s):
        return [(link_h[which, s, k], link_l[which, s, k]) for k in range(3)]

    def mapping(which):
        return [(map_h[which, k], map_l[which, k]) for k in range(3)]

    def three(ref, *at):
        return split3(ref[(*at, 0)], ref[(*at, 1)])

    def sandwiches(*jobs):
        for slot, (outer, state, _) in enumerate(jobs):
            tmp[slot, 0], tmp[slot, 1] = cprod(state(), outer(), transposed=True)
        for slot, (outer, _, write) in enumerate(jobs):
            write(*cprod(outer(), three(tmp, slot)))

    def added(target, at, *terms):
        def write(real, imag):
            for part, value in enumerate((real, imag)):
                target[(*at, part)] = value + sum(ref[(*where, part)] for ref, where in terms)

        return write

    def make_links(s, *pairs):
        factor = three(cpl, s)
        for which, ref, at in pairs:
            keep(link_h, link_l, (which, s), cprod(three(ref, *at), factor))

    def make_sources(s, *pairs):
        scale = orb[pl.ds(s, 1), :]
        for which, ref, at in pairs:
            real, imag = ref[(*at, 0)], ref[(*at, 1)]
            made = cprod(split3(real * scale, imag * scale), split3(real, imag))
            src[which, s, 0], src[which, s, 1] = real + made[0], imag + made[1]

    @pl.loop(0, slabs)
    def _(s):
        make_links(s, (2, g, (s,)))

    for copy in halos:
        copy.wait()
    for index, (ref, pad) in enumerate(((pot, pad_f), (perm, pad_p))):
        pad[1 : n0 + 1, 1 : n1 + 1, :] = ref[...]
        pad[1 : n0 + 1, 0:1, :] = jnp.where(e > 0, hr_before[index], 0.0)
        pad[1 : n0 + 1, n1 + 1 : n1 + 2, :] = jnp.where(e < ne - 1, hr_after[index], 0.0)
        pad[0, 1 : n1 + 1, :] = jnp.where(z > 0, zr_before[index], 0.0)
        pad[n0 + 1, 1 : n1 + 1, :] = jnp.where(z < nz - 1, zr_after[index], 0.0)
    centre = perm[...]
    field = pot[...]
    lane = lax.broadcasted_iota(jnp.int32, (n0, n1, n2), 2)
    inner0, inner1 = slice(1, n0 + 1), slice(1, n1 + 1)
    windows = [
        (pad_f[2 : n0 + 2, inner1, :], pad_p[2 : n0 + 2, inner1, :]),
        (pad_f[0:n0, inner1, :], pad_p[0:n0, inner1, :]),
        (pad_f[inner0, 2 : n1 + 2, :], pad_p[inner0, 2 : n1 + 2, :]),
        (pad_f[inner0, 0:n1, :], pad_p[inner0, 0:n1, :]),
    ]
    for shift, edge in ((n2 - 1, n2 - 1), (1, 0)):
        windows.append(
            tuple(jnp.where(lane == edge, 0.0, pltpu.roll(x, shift, 2)) for x in (field, centre))
        )
    load_small[2].wait()
    load_small[3].wait()
    numerator = charge[...]
    denominator = jnp.zeros_like(numerator)
    for near_field, near_perm in windows:
        face = 0.5 * (centre + near_perm)
        numerator = numerator + face * near_field
        denominator = denominator + face
    swept = numerator / denominator
    pot_out[...] = swept
    for plane in range(n0):
        cells[pl.ds(plane * n1, n1), :] = swept[plane]

    depth_bits = int(math.log2(n2))
    cross_bits = int(math.log2(n1 * ne))
    rows = slab_cells * n1
    for s in range(slabs):
        index = owner[s : s + 1, :]
        first = index >> (depth_bits + cross_bits)
        second = ((index >> depth_bits) & (n1 * ne - 1)) - e * n1
        third = index & (n2 - 1)
        chosen = jnp.where(
            lax.broadcasted_iota(jnp.int32, (n2, n), 0) == third, 1.0, 0.0
        ).astype(BF16)
        block = cells[pl.ds(s * rows, rows), :]
        high, low = split(block)
        lowest = (block - high.astype(F32) - low.astype(F32)).astype(BF16)
        picked = sum(
            jnp.dot(piece, chosen, preferred_element_type=F32) for piece in (high, low, lowest)
        )
        here = (second >= 0) & (second < n1)
        at = jnp.where(here, first * n1 + second, -1)
        mine = lax.broadcasted_iota(jnp.int32, (rows, n), 0) == at
        ar_loc[s : s + 1, :] = jnp.sum(jnp.where(mine, picked, 0.0), axis=0, keepdims=True)

    row_copies = [remote(ar_loc, ar_row.at[k - 1], ROW + k - 1, in_row(k)) for k in range(1, row)]
    for copy in row_copies:
        copy.start()

    tmp[0, 0], tmp[0, 1] = cprod(link(2, 1), link(2, 0))
    keep(map_h, map_l, (HALF,), cprod(link(2, 3), link(2, 2)))
    p_own[0], p_own[1] = cprod(mapping(HALF), three(tmp, 0))

    send_p = remote(p_own, p_even, PAIR, level(1))

    @pl.when(jnp.logical_and(jnp.logical_not(odd), z > 0))
    def _():
        send_p.start()

    for copy in row_copies:
        copy.wait()
    total = ar_loc[...]
    for k in range(1, row):
        total = total + ar_row[k - 1]
    ar_mid[...] = total
    col_copies = [
        remote(ar_mid, ar_col.at[k - 1], COL + k - 1, energy(row * k)) for k in range(1, cols)
    ]
    for copy in col_copies:
        copy.start()
    for copy in col_copies:
        copy.wait()
    total = ar_mid[...]
    for k in range(1, cols):
        total = total + ar_col[k - 1]
    orb[...] = total

    for s in range(1, slabs):
        g_copy(s, True).start()
        g_copy(s, False).start()

    @pl.loop(0, slabs)
    def _(s):
        make_sources(s, (2, g, (s,)))

    sandwiches(
        (lambda: link(2, 1), lambda: three(src, 2, 0), added(base, (), (src, (2, 1)))),
        (lambda: link(2, 3), lambda: three(src, 2, 2), added(k_out, (), (src, (2, 3)))),
    )
    sandwiches((lambda: mapping(HALF), lambda: three(base), added(s_own, (), (k_out, ()))))

    send_s = remote(s_own, s_even, PAIR + 1, level(1))

    @pl.when(jnp.logical_not(odd))
    def _():
        send_s.start()

    def make_weights():
        load_t.wait()
        for offset in (1, 2):
            raise_now = jnp.zeros((n, n), F32)
            lower_now = jnp.zeros((n, n), F32)
            for mode in range(tiles.shape[0]):
                hit = jnp.where(shifts[mode] == offset, 1.0, 0.0)
                raise_now = raise_now + (hit * occ[mode]) * tiles[mode]
                lower_now = lower_now + (hit * (occ[mode] + 1.0)) * tiles[mode]
            raise_now = jnp.where(e + offset < ne, raise_now, 0.0)
            lower_now = jnp.where(e >= offset, lower_now, 0.0)
            if offset == 2:
                weight[0], weight[1] = lower_now, raise_now
            else:
                weight[2] = jnp.where(core == 0, raise_now, lower_now)
                weight[3] = jnp.where(core == 0, lower_now, raise_now)

    def prepare_neighbours(first, last):
        def one(s, nothing):
            for side in range(2):
                g_copy(s, side == 0).wait_recv()
            both = [(side, g_nb, (side, s)) for side in range(2)]
            make_links(s, *both)
            make_sources(s, *both)

            @pl.when(s > 1)
            def _():
                sandwiches(
                    *(
                        (
                            lambda side=side: link(side, s),
                            lambda side=side: three(src, side, s - 1),
                            added(src, (side, s), (src, (side, s))),
                        )
                        for side in range(2)
                    )
                )
                for side in range(2):
                    keep(link_h, link_l, (side, s), cprod(link(side, s), link(side, s - 1)))

            return nothing

        lax.fori_loop(first, last, one, 0)

    make_weights()

    def k_slices():
        rows_each = n // (K_PIECES // 2)
        return [
            (part, pl.ds(h * rows_each, rows_each))
            for h in range(K_PIECES // 2)
            for part in range(2)
        ]

    def k_piece(source, first, i, device):
        at = k_slices()[i]
        return remote(source.at[at], k_in.at[at], first + i, device)

    pieces = range(K_PIECES)
    k_up = [k_piece(k_out, KUP, i, level(2)) for i in pieces]
    k_down = [k_piece(k_in, KDOWN, i, level(-1)) for i in pieces]
    k_side = [k_piece(k_in, KSIDE, i, level(1)) for i in pieces]
    through_ring = range(K_AHEAD, K_PIECES)
    k_back = {i: k_piece(k_out, KBACK, i, level(-2)) for i in through_ring}
    k_relay = {i: k_piece(k_in, KBACK, i, level(-2)) for i in through_ring}
    ahead = [
        remote(p_even, map_in, AHEAD, level(1)),
        remote(s_own, state_in, AHEAD + 1, level(1)),
    ]
    ahead_relay = [
        remote(map_in, map_in, AHEAD, level(1)),
        remote(state_in, state_in, AHEAD + 1, level(1)),
    ]

    def pair_state():
        keep(map_h, map_l, (ODD,), (p_own[0], p_own[1]))
        send_s.wait_recv()
        sandwiches((lambda: mapping(ODD), lambda: three(s_even), added(s_own, (), (s_own, ()))))

    def pair_maps():
        send_p.wait_recv()
        keep(map_h, map_l, (EVEN,), (p_even[0], p_even[1]))

    def own_green(s, outer, ref, at, term):
        sandwiches((outer, lambda: three(ref, *at), added(greens, (s,), term)))

    def map_through(which):
        keep(map_h, map_l, (FIRST,), cprod(link(2, 0), mapping(which)))

    def add_through(state):
        sandwiches(
            (lambda: link(2, 0), lambda: three(state), added(base, (), (src, (2, 0))))
        )

    def first_green():
        own_green(0, lambda: mapping(FIRST), k_in, (), (base, ()))

    def receive_and_hand_on(copies, *onward, these=pieces):
        for i in these:
            copies[i].wait_recv()
            for copy in onward:
                copy[i].start()

    early = jnp.where(z >= 6, slabs - 1, jnp.where(odd, 1, slabs))

    @pl.when(z == 0)
    def _():
        greens[0] = src[2, 0]

    @pl.when(z == 1)
    def _():
        pair_state()
        k_out[...] = s_own[...]
        for copy in k_up:
            copy.start()
        own_green(0, lambda: link(2, 0), s_even, (), (src, (2, 0)))

    @pl.when(jnp.logical_or(z == 3, z == 5))
    def _():
        pair_maps()
        keep(map_h, map_l, (ODD,), (p_own[0], p_own[1]))
        both = cprod(mapping(ODD), mapping(EVEN))

        @pl.when(z == 3)
        def _():
            keep(map_h, map_l, (BOTH,), both)

        @pl.when(z == 5)
        def _():
            p_even[0], p_even[1] = both
            ahead[0].start()

        pair_state()

        @pl.when(z == 5)
        def _():
            ahead[1].start()

        map_through(EVEN)
        add_through(s_even)

    @pl.when(z == 7)
    def _():
        pair_maps()
        send_s.wait_recv()
        ahead[0].wait_recv()
        keep(map_h, map_l, (BOTH,), cprod(mapping(EVEN), three(map_in)))
        map_through(BOTH)

    @pl.when(z == 6)
    def _():
        for copy, relay in zip(ahead, ahead_relay):
            copy.wait_recv()
            relay.start()
        keep(map_h, map_l, (BOTH,), (map_in[0], map_in[1]))
        map_through(BOTH)
        add_through(state_in)

    prepare_neighbours(1, early)

    @pl.when(z == 3)
    def _():
        receive_and_hand_on(k_up, k_down)
        sandwiches((lambda: mapping(BOTH), lambda: three(k_in), added(k_out, (), (s_own, ()))))
        for i in pieces:
            k_up[i].start()
        for i in through_ring:
            k_back[i].start()

    @pl.when(z == 5)
    def _():
        receive_and_hand_on(k_up, k_side, k_down)

    @pl.when(jnp.logical_or(z == 3, z == 5))
    def _():
        first_green()

    @pl.when(z == 7)
    def _():
        ahead[1].wait_recv()
        sandwiches(
            (lambda: mapping(EVEN), lambda: three(state_in), added(k_out, (), (s_even, ())))
        )
        add_through(k_out)
        receive_and_hand_on(k_side, these=range(K_AHEAD))
        receive_and_hand_on(k_back, these=through_ring)
        first_green()

    @pl.when(jnp.logical_or(z == 2, z == 4))
    def _():
        receive_and_hand_on(k_down)
        own_green(0, lambda: link(2, 0), k_in, (), (src, (2, 0)))

    @pl.when(z == 6)
    def _():
        receive_and_hand_on(k_side, k_side, these=range(K_AHEAD))
        receive_and_hand_on(k_side, these=through_ring)
        first_green()

    def first_copy(side):
        return remote(
            greens.at[0],
            greens_nb.at[side, 0],
            CARRY + side,
            energy(2 if side == 0 else -2),
        )

    def own_copy(s):
        return remote(greens.at[s], sib_own.at[s], SIB + s, sibling)

    for side in range(2):
        first_copy(side).start()
    own_copy(0).start()

    @pl.loop(1, slabs)
    def _(s):
        own_green(s, lambda: link(2, s), greens, (s - 1,), (src, (2, s)))
        own_copy(s).start()

    @pl.when(z == 1)
    def _():
        receive_and_hand_on(k_back, k_relay, these=through_ring)

    prepare_neighbours(early, slabs)

    def far_copy(side, s):
        return remote(greens_nb.at[side, s], sib_nb.at[s], SIBN + s, sibling)

    def far_greens(side, use):
        def write(s):
            return lambda *made: use(s, *(made[part] + src[side, s, part] for part in range(2)))

        sandwiches(
            *(
                (lambda s=s: link(side, s), lambda: three(greens_nb, side, 0), write(s))
                for s in range(1, slabs)
            )
        )

    def mix_most(s, part, near):
        se_out[0, s, part] = (
            weight[core] * near
            + weight[1 - core] * greens_nb[1 - core, s, part]
            + weight[2] * sib_own[s, part]
        )

    for side in range(2):
        first_copy(side).wait_recv()
    far_copy(1 - core, 0).start()

    def store_and_send(s, real, imag):
        greens_nb[1 - core, s, 0], greens_nb[1 - core, s, 1] = real, imag
        far_copy(1 - core, s).start()

    def mix_both(s, real, imag):
        mix_most(s, 0, real)
        mix_most(s, 1, imag)

    far_greens(1 - core, store_and_send)
    for s in range(slabs):
        own_copy(s).wait_recv()
    mix_both(0, greens_nb[core, 0, 0], greens_nb[core, 0, 1])
    far_greens(core, mix_both)

    @pl.loop(0, slabs)
    def _(s):
        far_copy(0, s).wait_recv()
        for part in range(2):
            se_out[0, s, part] = se_out[0, s, part] + weight[3] * sib_nb[s, part]

    for s in range(slabs):
        own_copy(s).wait_send()
        far_copy(0, s).wait_send()
    for s in range(1, slabs):
        g_copy(s, True).wait_send()
        g_copy(s, False).wait_send()
    for side in range(2):
        first_copy(side).wait_send()

    def sent(condition, *copies):
        @pl.when(condition)
        def _():
            for copy in copies:
                copy.wait_send()

    sent(jnp.logical_not(odd), send_s)
    sent(jnp.logical_and(jnp.logical_not(odd), z > 0), send_p)
    sent(jnp.logical_or(z == 1, z == 3), *k_up)
    sent(jnp.logical_or(z == 3, z == 5), *k_down)
    sent(z == 5, *k_side)
    sent(z == 6, *k_side[:K_AHEAD])
    sent(z == 3, *k_back.values())
    sent(z == 1, *k_relay.values())
    sent(z == 5, *ahead)
    sent(z == 6, *ahead_relay)


def per_device(
    ne,
    nz,
    potential_old,
    charge,
    permittivity,
    owner_cell,
    green_free,
    coupling,
    shifts,
    occupation,
    mode_tiles,
):
    n0, n1, n2 = potential_old.shape
    slabs, n = owner_cell.shape
    modes = mode_tiles.shape[0]
    vmem = pl.BlockSpec(memory_space=pltpu.VMEM)
    smem = pl.BlockSpec(memory_space=pltpu.SMEM)
    hbm = pl.BlockSpec(memory_space=pl.ANY)
    row = min(8, ne)
    cols = ne // row
    block = (2, n, n)
    sems = 4 + row - 1 + cols - 1 + 2 * slabs + 2 + 3 * K_PIECES + 2 + 2 + 2 * slabs
    scratch = [
        pltpu.VMEM((n0, n1, n2), F32),
        pltpu.VMEM((n0, n1, n2), F32),
        pltpu.VMEM((n0, n1, n2), F32),
        pltpu.VMEM((slabs, n), jnp.int32),
        pltpu.VMEM((slabs,) + block, F32),
        pltpu.VMEM((slabs,) + block, F32),
        pltpu.VMEM((modes, n, n), F32),
        pltpu.VMEM((2, n0, 1, n2), F32),
        pltpu.VMEM((2, n0, 1, n2), F32),
        pltpu.VMEM((2, n1, n2), F32),
        pltpu.VMEM((2, n1, n2), F32),
        pltpu.VMEM((2, n0, 1, n2), F32),
        pltpu.VMEM((2, n0, 1, n2), F32),
        pltpu.VMEM((2, n1, n2), F32),
        pltpu.VMEM((2, n1, n2), F32),
        pltpu.VMEM((n0 + 2, 8, n2), F32),
        pltpu.VMEM((n0 + 2, 8, n2), F32),
        pltpu.VMEM((n0 * n1, n2), F32),
        pltpu.VMEM((slabs, n), F32),
        pltpu.VMEM((slabs, n), F32),
        pltpu.VMEM((row, slabs, n), F32),
        pltpu.VMEM((cols, slabs, n), F32),
        pltpu.VMEM((slabs, n), F32),
        pltpu.VMEM((2, slabs) + block, F32),
        pltpu.VMEM((3, slabs, 3, n, n), BF16),
        pltpu.VMEM((3, slabs, 3, n, n), BF16),
        pltpu.VMEM((3, slabs) + block, F32),
        pltpu.VMEM(block, F32),
        pltpu.VMEM(block, F32),
        pltpu.VMEM(block, F32),
        pltpu.VMEM(block, F32),
        pltpu.VMEM((5, 3, n, n), BF16),
        pltpu.VMEM((5, 3, n, n), BF16),
        pltpu.VMEM((3,) + block, F32),
        pltpu.VMEM(block, F32),
        pltpu.VMEM(block, F32),
        pltpu.VMEM(block, F32),
        pltpu.VMEM(block, F32),
        pltpu.VMEM(block, F32),
        pltpu.VMEM((slabs,) + block, F32),
        pltpu.VMEM((2, slabs) + block, F32),
        pltpu.VMEM((slabs,) + block, F32),
        pltpu.VMEM((slabs,) + block, F32),
        pltpu.VMEM((4, n, n), F32),
        pltpu.SemaphoreType.DMA((sems,)),
        pltpu.SemaphoreType.DMA((sems,)),
        pltpu.SemaphoreType.DMA((7,)),
    ]
    return pl.pallas_call(
        functools.partial(kernel, ne, nz),
        out_shape=(
            pltpu.VMEM((n0, n1, n2), F32),
            pltpu.VMEM((1, slabs) + block, F32),
        ),
        in_specs=[hbm, hbm, hbm, hbm, hbm, hbm, smem, smem, hbm],
        out_specs=(vmem, vmem),
        scratch_shapes=scratch,
        compiler_params=pltpu.CompilerParams(
            collective_id=0, has_side_effects=True, vmem_limit_bytes=54 << 20
        ),
    )(
        potential_old,
        charge,
        permittivity,
        owner_cell,
        green_free,
        coupling,
        shifts,
        occupation,
        mode_tiles,
    )


def solution(mesh):
    in_specs = (
        P("slab", "energy", None),
        P("slab", "energy", None),
        P("slab", "energy", None),
        P("slab", None),
        P("energy", "slab", None, None, None),
        P("slab", None, None, None),
        P(),
        P(),
        P(),
    )
    out_specs = (P("slab", "energy", None), P("energy", "slab", None, None, None))
    return jax.shard_map(
        functools.partial(per_device, mesh.shape["energy"], mesh.shape["slab"]),
        mesh=mesh,
        in_specs=in_specs,
        out_specs=out_specs,
        check_vma=False,
    )
```

```python
import functools
import math

import jax
import jax.numpy as jnp
from jax import lax
from jax.experimental import pallas as pl
from jax.experimental.pallas import tpu as pltpu
from jax.sharding import PartitionSpec as P

F32 = jnp.float32
BF16 = jnp.bfloat16
MESH = pl.DeviceIdType.MESH
K_PIECES = 8
K_AHEAD = 1


def split(x):
    high = x.astype(BF16)
    return high, (x - high.astype(F32)).astype(BF16)


def split3(real, imag):
    return split(real), split(imag), split(real + imag)


def cprod(left, right, transposed=False):
    dims = (((1,), (1 if transposed else 0,)), ((), ()))
    dot = functools.partial(lax.dot_general, dimension_numbers=dims, preferred_element_type=F32)
    first, second, third = (
        dot(a[0], b[0]) + dot(a[1], b[0]) + dot(a[0], b[1]) for a, b in zip(left, right)
    )
    return first - second, third - first - second


def kernel(
    ne,
    nz,
    pot_hbm,
    charge_hbm,
    perm_hbm,
    owner_hbm,
    g_hbm,
    cpl_hbm,
    shifts,
    occ,
    tiles_hbm,
    pot_out,
    se_out,
    pot,
    charge,
    perm,
    owner,
    g,
    cpl,
    tiles,
    hs_lo,
    hs_hi,
    zs_lo,
    zs_hi,
    hr_before,
    hr_after,
    zr_before,
    zr_after,
    pad_f,
    pad_p,
    cells,
    ar_loc,
    ar_mid,
    ar_row,
    ar_col,
    orb,
    g_nb,
    link_h,
    link_l,
    src,
    p_own,
    s_own,
    p_even,
    s_even,
    map_h,
    map_l,
    tmp,
    map_in,
    state_in,
    k_in,
    k_out,
    base,
    greens,
    greens_nb,
    sib_own,
    sib_nb,
    weight,
    send_sem,
    recv_sem,
    local_sem,
):
    n0, n1, n2 = pot.shape
    slabs, n = owner.shape
    slab_cells = n0 // slabs
    assert (nz, slabs) == (8, 4)
    row = min(8, ne)
    cols = ne // row
    e, z = lax.axis_index("energy"), lax.axis_index("slab")
    core = lax.rem(e, 2)
    sibling = (e + 1 - 2 * core, z)
    odd = lax.rem(z, 2) == 1

    def energy(by):
        return (lax.rem(e + (by + ne), ne), z)

    def level(by):
        return (e, lax.rem(z + (by + nz), nz))

    def in_row(k):
        base = (e // row) * row
        return (base + lax.rem(e - base + k, row), z)

    def remote(source, target, index, device):
        return pltpu.make_async_remote_copy(
            src_ref=source,
            dst_ref=target,
            send_sem=send_sem.at[index],
            recv_sem=recv_sem.at[index],
            device_id=device,
            device_id_type=MESH,
        )

    HALO, ROW = 0, 4
    COL = ROW + row - 1
    GEX = COL + cols - 1
    PAIR = GEX + 2 * slabs
    KUP, KDOWN, KBACK = (PAIR + 2 + i * K_PIECES for i in range(3))
    KSIDE = KUP
    AHEAD = KBACK + K_PIECES
    CARRY = AHEAD + 2
    SIB = CARRY + 2
    SIBN = SIB + slabs

    load_small = [
        pltpu.make_async_copy(source, target, local_sem.at[3 + i])
        for i, (source, target) in enumerate(
            ((pot_hbm, pot), (perm_hbm, perm), (charge_hbm, charge), (owner_hbm, owner))
        )
    ]
    for copy in load_small:
        copy.start()
    load_g = pltpu.make_async_copy(g_hbm.at[0], g, local_sem.at[0])
    load_c = pltpu.make_async_copy(cpl_hbm, cpl, local_sem.at[1])
    load_t = pltpu.make_async_copy(tiles_hbm, tiles, local_sem.at[2])
    partners = [in_row(k) for k in range(1, row)] + [energy(row * k) for k in range(1, cols)]
    partners += [energy(by) for by in (1, -1, 2, -2)] + [level(by) for by in (1, -1, 2, -2)]
    barrier = pltpu.get_barrier_semaphore()
    for device in partners:
        pl.semaphore_signal(barrier, inc=1, device_id=device, device_id_type=MESH)

    load_g.start()
    load_c.start()
    load_t.start()
    load_small[0].wait()
    load_small[1].wait()
    for index, ref in enumerate((pot, perm)):
        hs_lo[index] = ref[:, 0:1, :]
        hs_hi[index] = ref[:, n1 - 1 : n1, :]
        zs_lo[index] = ref[0]
        zs_hi[index] = ref[n0 - 1]
    pl.semaphore_wait(barrier, len(partners))

    halos = [
        remote(hs_lo, hr_after, HALO, energy(-1)),
        remote(hs_hi, hr_before, HALO + 1, energy(1)),
        remote(zs_lo, zr_after, HALO + 2, level(-1)),
        remote(zs_hi, zr_before, HALO + 3, level(1)),
    ]
    for copy in halos:
        copy.start()

    load_g.wait()

    def g_copy(s, to_upper):
        side = 0 if to_upper else 1
        return remote(
            g.at[s], g_nb.at[side, s], GEX + side * slabs + s, energy(2 if to_upper else -2)
        )

    load_c.wait()
    EVEN, ODD, BOTH, HALF, FIRST = range(5)

    def keep(high, low, at, parts):
        for k, (h, l) in enumerate(split3(*parts)):
            high[(*at, k)], low[(*at, k)] = h, l

    def link(which, s):
        return [(link_h[which, s, k], link_l[which, s, k]) for k in range(3)]

    def mapping(which):
        return [(map_h[which, k], map_l[which, k]) for k in range(3)]

    def three(ref, *at):
        return split3(ref[(*at, 0)], ref[(*at, 1)])

    def sandwiches(*jobs):
        for slot, (outer, state, _) in enumerate(jobs):
            tmp[slot, 0], tmp[slot, 1] = cprod(state(), outer(), transposed=True)
        for slot, (outer, _, write) in enumerate(jobs):
            write(*cprod(outer(), three(tmp, slot)))

    def added(target, at, *terms):
        def write(real, imag):
            for part, value in enumerate((real, imag)):
                target[(*at, part)] = value + sum(ref[(*where, part)] for ref, where in terms)

        return write

    def make_links(s, *pairs):
        factor = three(cpl, s)
        for which, ref, at in pairs:
            keep(link_h, link_l, (which, s), cprod(three(ref, *at), factor))

    def make_sources(s, *pairs):
        scale = orb[pl.ds(s, 1), :]
        for which, ref, at in pairs:
            real, imag = ref[(*at, 0)], ref[(*at, 1)]
            made = cprod(split3(real * scale, imag * scale), split3(real, imag))
            src[which, s, 0], src[which, s, 1] = real + made[0], imag + made[1]

    @pl.loop(0, slabs)
    def _(s):
        make_links(s, (2, g, (s,)))

    for copy in halos:
        copy.wait()
    for index, (ref, pad) in enumerate(((pot, pad_f), (perm, pad_p))):
        pad[1 : n0 + 1, 1 : n1 + 1, :] = ref[...]
        pad[1 : n0 + 1, 0:1, :] = jnp.where(e > 0, hr_before[index], 0.0)
        pad[1 : n0 + 1, n1 + 1 : n1 + 2, :] = jnp.where(e < ne - 1, hr_after[index], 0.0)
        pad[0, 1 : n1 + 1, :] = jnp.where(z > 0, zr_before[index], 0.0)
        pad[n0 + 1, 1 : n1 + 1, :] = jnp.where(z < nz - 1, zr_after[index], 0.0)
    centre = perm[...]
    field = pot[...]
    lane = lax.broadcasted_iota(jnp.int32, (n0, n1, n2), 2)
    inner0, inner1 = slice(1, n0 + 1), slice(1, n1 + 1)
    windows = [
        (pad_f[2 : n0 + 2, inner1, :], pad_p[2 : n0 + 2, inner1, :]),
        (pad_f[0:n0, inner1, :], pad_p[0:n0, inner1, :]),
        (pad_f[inner0, 2 : n1 + 2, :], pad_p[inner0, 2 : n1 + 2, :]),
        (pad_f[inner0, 0:n1, :], pad_p[inner0, 0:n1, :]),
    ]
    for shift, edge in ((n2 - 1, n2 - 1), (1, 0)):
        windows.append(
            tuple(jnp.where(lane == edge, 0.0, pltpu.roll(x, shift, 2)) for x in (field, centre))
        )
    load_small[2].wait()
    load_small[3].wait()
    numerator = charge[...]
    denominator = jnp.zeros_like(numerator)
    for near_field, near_perm in windows:
        face = 0.5 * (centre + near_perm)
        numerator = numerator + face * near_field
        denominator = denominator + face
    swept = numerator / denominator
    pot_out[...] = swept
    for plane in range(n0):
        cells[pl.ds(plane * n1, n1), :] = swept[plane]

    depth_bits = int(math.log2(n2))
    cross_bits = int(math.log2(n1 * ne))
    rows = slab_cells * n1
    for s in range(slabs):
        index = owner[s : s + 1, :]
        first = index >> (depth_bits + cross_bits)
        second = ((index >> depth_bits) & (n1 * ne - 1)) - e * n1
        third = index & (n2 - 1)
        chosen = jnp.where(
            lax.broadcasted_iota(jnp.int32, (n2, n), 0) == third, 1.0, 0.0
        ).astype(BF16)
        block = cells[pl.ds(s * rows, rows), :]
        high, low = split(block)
        lowest = (block - high.astype(F32) - low.astype(F32)).astype(BF16)
        picked = sum(
            jnp.dot(piece, chosen, preferred_element_type=F32) for piece in (high, low, lowest)
        )
        here = (second >= 0) & (second < n1)
        at = jnp.where(here, first * n1 + second, -1)
        mine = lax.broadcasted_iota(jnp.int32, (rows, n), 0) == at
        ar_loc[s : s + 1, :] = jnp.sum(jnp.where(mine, picked, 0.0), axis=0, keepdims=True)

    row_copies = [remote(ar_loc, ar_row.at[k - 1], ROW + k - 1, in_row(k)) for k in range(1, row)]
    for copy in row_copies:
        copy.start()

    tmp[0, 0], tmp[0, 1] = cprod(link(2, 1), link(2, 0))
    keep(map_h, map_l, (HALF,), cprod(link(2, 3), link(2, 2)))
    p_own[0], p_own[1] = cprod(mapping(HALF), three(tmp, 0))

    send_p = remote(p_own, p_even, PAIR, level(1))

    @pl.when(jnp.logical_and(jnp.logical_not(odd), z > 0))
    def _():
        send_p.start()

    for copy in row_copies:
        copy.wait()
    total = ar_loc[...]
    for k in range(1, row):
        total = total + ar_row[k - 1]
    ar_mid[...] = total
    col_copies = [
        remote(ar_mid, ar_col.at[k - 1], COL + k - 1, energy(row * k)) for k in range(1, cols)
    ]
    for copy in col_copies:
        copy.start()
    for copy in col_copies:
        copy.wait()
    total = ar_mid[...]
    for k in range(1, cols):
        total = total + ar_col[k - 1]
    orb[...] = total

    for s in range(1, slabs):
        g_copy(s, True).start()
        g_copy(s, False).start()

    @pl.loop(0, slabs)
    def _(s):
        make_sources(s, (2, g, (s,)))

    sandwiches(
        (lambda: link(2, 1), lambda: three(src, 2, 0), added(base, (), (src, (2, 1)))),
        (lambda: link(2, 3), lambda: three(src, 2, 2), added(k_out, (), (src, (2, 3)))),
    )
    sandwiches((lambda: mapping(HALF), lambda: three(base), added(s_own, (), (k_out, ()))))

    send_s = remote(s_own, s_even, PAIR + 1, level(1))

    @pl.when(jnp.logical_not(odd))
    def _():
        send_s.start()

    def make_weights():
        load_t.wait()
        for offset in (1, 2):
            raise_now = jnp.zeros((n, n), F32)
            lower_now = jnp.zeros((n, n), F32)
            for mode in range(tiles.shape[0]):
                hit = jnp.where(shifts[mode] == offset, 1.0, 0.0)
                raise_now = raise_now + (hit * occ[mode]) * tiles[mode]
                lower_now = lower_now + (hit * (occ[mode] + 1.0)) * tiles[mode]
            raise_now = jnp.where(e + offset < ne, raise_now, 0.0)
            lower_now = jnp.where(e >= offset, lower_now, 0.0)
            if offset == 2:
                weight[0], weight[1] = lower_now, raise_now
            else:
                weight[2] = jnp.where(core == 0, raise_now, lower_now)
                weight[3] = jnp.where(core == 0, lower_now, raise_now)

    def prepare_neighbours(first, last):
        def one(s, nothing):
            for side in range(2):
                g_copy(s, side == 0).wait_recv()
            both = [(side, g_nb, (side, s)) for side in range(2)]
            make_links(s, *both)
            make_sources(s, *both)

            @pl.when(s > 1)
            def _():
                sandwiches(
                    *(
                        (
                            lambda side=side: link(side, s),
                            lambda side=side: three(src, side, s - 1),
                            added(src, (side, s), (src, (side, s))),
                        )
                        for side in range(2)
                    )
                )
                for side in range(2):
                    keep(link_h, link_l, (side, s), cprod(link(side, s), link(side, s - 1)))

            return nothing

        lax.fori_loop(first, last, one, 0)

    make_weights()

    def k_slices():
        rows_each = n // (K_PIECES // 2)
        return [
            (part, pl.ds(h * rows_each, rows_each))
            for h in range(K_PIECES // 2)
            for part in range(2)
        ]

    def k_piece(source, first, i, device):
        at = k_slices()[i]
        return remote(source.at[at], k_in.at[at], first + i, device)

    pieces = range(K_PIECES)
    k_up = [k_piece(k_out, KUP, i, level(2)) for i in pieces]
    k_down = [k_piece(k_in, KDOWN, i, level(-1)) for i in pieces]
    k_side = [k_piece(k_in, KSIDE, i, level(1)) for i in pieces]
    through_ring = range(K_AHEAD, K_PIECES)
    k_back = {i: k_piece(k_out, KBACK, i, level(-2)) for i in through_ring}
    k_relay = {i: k_piece(k_in, KBACK, i, level(-2)) for i in through_ring}
    ahead = [
        remote(p_even, map_in, AHEAD, level(1)),
        remote(s_own, state_in, AHEAD + 1, level(1)),
    ]
    ahead_relay = [
        remote(map_in, map_in, AHEAD, level(1)),
        remote(state_in, state_in, AHEAD + 1, level(1)),
    ]

    def pair_state():
        keep(map_h, map_l, (ODD,), (p_own[0], p_own[1]))
        send_s.wait_recv()
        sandwiches((lambda: mapping(ODD), lambda: three(s_even), added(s_own, (), (s_own, ()))))

    def pair_maps():
        send_p.wait_recv()
        keep(map_h, map_l, (EVEN,), (p_even[0], p_even[1]))

    def own_green(s, outer, ref, at, term):
        sandwiches((outer, lambda: three(ref, *at), added(greens, (s,), term)))

    def map_through(which):
        keep(map_h, map_l, (FIRST,), cprod(link(2, 0), mapping(which)))

    def add_through(state):
        sandwiches(
            (lambda: link(2, 0), lambda: three(state), added(base, (), (src, (2, 0))))
        )

    def first_green():
        own_green(0, lambda: mapping(FIRST), k_in, (), (base, ()))

    def receive_and_hand_on(copies, *onward, these=pieces):
        for i in these:
            copies[i].wait_recv()
            for copy in onward:
                copy[i].start()

    early = jnp.where(z >= 6, slabs - 1, jnp.where(odd, 1, slabs))

    @pl.when(z == 0)
    def _():
        greens[0] = src[2, 0]

    @pl.when(z == 1)
    def _():
        pair_state()
        k_out[...] = s_own[...]
        for copy in k_up:
            copy.start()
        own_green(0, lambda: link(2, 0), s_even, (), (src, (2, 0)))

    @pl.when(jnp.logical_or(z == 3, z == 5))
    def _():
        pair_maps()
        keep(map_h, map_l, (ODD,), (p_own[0], p_own[1]))
        both = cprod(mapping(ODD), mapping(EVEN))

        @pl.when(z == 3)
        def _():
            keep(map_h, map_l, (BOTH,), both)

        @pl.when(z == 5)
        def _():
            p_even[0], p_even[1] = both
            ahead[0].start()

        pair_state()

        @pl.when(z == 5)
        def _():
            ahead[1].start()

        map_through(EVEN)
        add_through(s_even)

    @pl.when(z == 7)
    def _():
        pair_maps()
        send_s.wait_recv()
        ahead[0].wait_recv()
        keep(map_h, map_l, (BOTH,), cprod(mapping(EVEN), three(map_in)))
        map_through(BOTH)

    @pl.when(z == 6)
    def _():
        for copy, relay in zip(ahead, ahead_relay):
            copy.wait_recv()
            relay.start()
        keep(map_h, map_l, (BOTH,), (map_in[0], map_in[1]))
        map_through(BOTH)
        add_through(state_in)

    prepare_neighbours(1, early)

    @pl.when(z == 3)
    def _():
        receive_and_hand_on(k_up, k_down)
        sandwiches((lambda: mapping(BOTH), lambda: three(k_in), added(k_out, (), (s_own, ()))))
        for i in through_ring:
            k_back[i].start()
        for i in pieces:
            k_up[i].start()

    @pl.when(z == 5)
    def _():
        receive_and_hand_on(k_up, k_side, k_down)

    @pl.when(jnp.logical_or(z == 3, z == 5))
    def _():
        first_green()

    @pl.when(z == 7)
    def _():
        ahead[1].wait_recv()
        sandwiches(
            (lambda: mapping(EVEN), lambda: three(state_in), added(k_out, (), (s_even, ())))
        )
        add_through(k_out)
        receive_and_hand_on(k_side, these=range(K_AHEAD))
        receive_and_hand_on(k_back, these=through_ring)
        first_green()

    @pl.when(jnp.logical_or(z == 2, z == 4))
    def _():
        receive_and_hand_on(k_down)
        own_green(0, lambda: link(2, 0), k_in, (), (src, (2, 0)))

    @pl.when(z == 6)
    def _():
        receive_and_hand_on(k_side, k_side, these=range(K_AHEAD))
        receive_and_hand_on(k_side, these=through_ring)
        first_green()

    def first_copy(side):
        return remote(
            greens.at[0],
            greens_nb.at[side, 0],
            CARRY + side,
            energy(2 if side == 0 else -2),
        )

    def own_copy(s):
        return remote(greens.at[s], sib_own.at[s], SIB + s, sibling)

    for side in range(2):
        first_copy(side).start()
    own_copy(0).start()

    @pl.loop(1, slabs)
    def _(s):
        own_green(s, lambda: link(2, s), greens, (s - 1,), (src, (2, s)))
        own_copy(s).start()

    @pl.when(z == 1)
    def _():
        receive_and_hand_on(k_back, k_relay, these=through_ring)

    prepare_neighbours(early, slabs)

    def far_copy(side, s):
        return remote(greens_nb.at[side, s], sib_nb.at[s], SIBN + s, sibling)

    def far_greens(side, use):
        def write(s):
            return lambda *made: use(s, *(made[part] + src[side, s, part] for part in range(2)))

        sandwiches(
            *(
                (lambda s=s: link(side, s), lambda: three(greens_nb, side, 0), write(s))
                for s in range(1, slabs)
            )
        )

    def mix_most(s, part, near):
        se_out[0, s, part] = (
            weight[core] * near
            + weight[1 - core] * greens_nb[1 - core, s, part]
            + weight[2] * sib_own[s, part]
        )

    for side in range(2):
        first_copy(side).wait_recv()
    far_copy(1 - core, 0).start()

    def store_and_send(s, real, imag):
        greens_nb[1 - core, s, 0], greens_nb[1 - core, s, 1] = real, imag
        far_copy(1 - core, s).start()

    def mix_both(s, real, imag):
        mix_most(s, 0, real)
        mix_most(s, 1, imag)

    far_greens(1 - core, store_and_send)
    for s in range(slabs):
        own_copy(s).wait_recv()
    mix_both(0, greens_nb[core, 0, 0], greens_nb[core, 0, 1])
    far_greens(core, mix_both)

    @pl.loop(0, slabs)
    def _(s):
        far_copy(0, s).wait_recv()
        for part in range(2):
            se_out[0, s, part] = se_out[0, s, part] + weight[3] * sib_nb[s, part]

    for s in range(slabs):
        own_copy(s).wait_send()
        far_copy(0, s).wait_send()
    for s in range(1, slabs):
        g_copy(s, True).wait_send()
        g_copy(s, False).wait_send()
    for side in range(2):
        first_copy(side).wait_send()

    def sent(condition, *copies):
        @pl.when(condition)
        def _():
            for copy in copies:
                copy.wait_send()

    sent(jnp.logical_not(odd), send_s)
    sent(jnp.logical_and(jnp.logical_not(odd), z > 0), send_p)
    sent(jnp.logical_or(z == 1, z == 3), *k_up)
    sent(jnp.logical_or(z == 3, z == 5), *k_down)
    sent(z == 5, *k_side)
    sent(z == 6, *k_side[:K_AHEAD])
    sent(z == 3, *k_back.values())
    sent(z == 1, *k_relay.values())
    sent(z == 5, *ahead)
    sent(z == 6, *ahead_relay)


def per_device(
    ne,
    nz,
    potential_old,
    charge,
    permittivity,
    owner_cell,
    green_free,
    coupling,
    shifts,
    occupation,
    mode_tiles,
):
    n0, n1, n2 = potential_old.shape
    slabs, n = owner_cell.shape
    modes = mode_tiles.shape[0]
    vmem = pl.BlockSpec(memory_space=pltpu.VMEM)
    smem = pl.BlockSpec(memory_space=pltpu.SMEM)
    hbm = pl.BlockSpec(memory_space=pl.ANY)
    row = min(8, ne)
    cols = ne // row
    block = (2, n, n)
    sems = 4 + row - 1 + cols - 1 + 2 * slabs + 2 + 3 * K_PIECES + 2 + 2 + 2 * slabs
    scratch = [
        pltpu.VMEM((n0, n1, n2), F32),
        pltpu.VMEM((n0, n1, n2), F32),
        pltpu.VMEM((n0, n1, n2), F32),
        pltpu.VMEM((slabs, n), jnp.int32),
        pltpu.VMEM((slabs,) + block, F32),
        pltpu.VMEM((slabs,) + block, F32),
        pltpu.VMEM((modes, n, n), F32),
        pltpu.VMEM((2, n0, 1, n2), F32),
        pltpu.VMEM((2, n0, 1, n2), F32),
        pltpu.VMEM((2, n1, n2), F32),
        pltpu.VMEM((2, n1, n2), F32),
        pltpu.VMEM((2, n0, 1, n2), F32),
        pltpu.VMEM((2, n0, 1, n2), F32),
        pltpu.VMEM((2, n1, n2), F32),
        pltpu.VMEM((2, n1, n2), F32),
        pltpu.VMEM((n0 + 2, 8, n2), F32),
        pltpu.VMEM((n0 + 2, 8, n2), F32),
        pltpu.VMEM((n0 * n1, n2), F32),
        pltpu.VMEM((slabs, n), F32),
        pltpu.VMEM((slabs, n), F32),
        pltpu.VMEM((row, slabs, n), F32),
        pltpu.VMEM((cols, slabs, n), F32),
        pltpu.VMEM((slabs, n), F32),
        pltpu.VMEM((2, slabs) + block, F32),
        pltpu.VMEM((3, slabs, 3, n, n), BF16),
        pltpu.VMEM((3, slabs, 3, n, n), BF16),
        pltpu.VMEM((3, slabs) + block, F32),
        pltpu.VMEM(block, F32),
        pltpu.VMEM(block, F32),
        pltpu.VMEM(block, F32),
        pltpu.VMEM(block, F32),
        pltpu.VMEM((5, 3, n, n), BF16),
        pltpu.VMEM((5, 3, n, n), BF16),
        pltpu.VMEM((3,) + block, F32),
        pltpu.VMEM(block, F32),
        pltpu.VMEM(block, F32),
        pltpu.VMEM(block, F32),
        pltpu.VMEM(block, F32),
        pltpu.VMEM(block, F32),
        pltpu.VMEM((slabs,) + block, F32),
        pltpu.VMEM((2, slabs) + block, F32),
        pltpu.VMEM((slabs,) + block, F32),
        pltpu.VMEM((slabs,) + block, F32),
        pltpu.VMEM((4, n, n), F32),
        pltpu.SemaphoreType.DMA((sems,)),
        pltpu.SemaphoreType.DMA((sems,)),
        pltpu.SemaphoreType.DMA((7,)),
    ]
    return pl.pallas_call(
        functools.partial(kernel, ne, nz),
        out_shape=(
            pltpu.VMEM((n0, n1, n2), F32),
            pltpu.VMEM((1, slabs) + block, F32),
        ),
        in_specs=[hbm, hbm, hbm, hbm, hbm, hbm, smem, smem, hbm],
        out_specs=(vmem, vmem),
        scratch_shapes=scratch,
        compiler_params=pltpu.CompilerParams(
            collective_id=0, has_side_effects=True, vmem_limit_bytes=54 << 20
        ),
    )(
        potential_old,
        charge,
        permittivity,
        owner_cell,
        green_free,
        coupling,
        shifts,
        occupation,
        mode_tiles,
    )


def solution(mesh):
    in_specs = (
        P("slab", "energy", None),
        P("slab", "energy", None),
        P("slab", "energy", None),
        P("slab", None),
        P("energy", "slab", None, None, None),
        P("slab", None, None, None),
        P(),
        P(),
        P(),
    )
    out_specs = (P("slab", "energy", None), P("energy", "slab", None, None, None))
    return jax.shard_map(
        functools.partial(per_device, mesh.shape["energy"], mesh.shape["slab"]),
        mesh=mesh,
        in_specs=in_specs,
        out_specs=out_specs,
        check_vma=False,
    )
```

```python
import functools
import math

import jax
import jax.numpy as jnp
from jax import lax
from jax.experimental import pallas as pl
from jax.experimental.pallas import tpu as pltpu
from jax.sharding import PartitionSpec as P

F32 = jnp.float32
BF16 = jnp.bfloat16
MESH = pl.DeviceIdType.MESH
K_PIECES = 16
K_AHEAD = 2


def split(x):
    high = x.astype(BF16)
    return high, (x - high.astype(F32)).astype(BF16)


def split3(real, imag):
    return split(real), split(imag), split(real + imag)


def cprod(left, right, transposed=False):
    dims = (((1,), (1 if transposed else 0,)), ((), ()))
    dot = functools.partial(lax.dot_general, dimension_numbers=dims, preferred_element_type=F32)
    first, second, third = (
        dot(a[0], b[0]) + dot(a[1], b[0]) + dot(a[0], b[1]) for a, b in zip(left, right)
    )
    return first - second, third - first - second


def kernel(
    ne,
    nz,
    pot_hbm,
    charge_hbm,
    perm_hbm,
    owner_hbm,
    g_hbm,
    cpl_hbm,
    shifts,
    occ,
    tiles_hbm,
    pot_out,
    se_out,
    pot,
    charge,
    perm,
    owner,
    g,
    cpl,
    tiles,
    hs_lo,
    hs_hi,
    zs_lo,
    zs_hi,
    hr_before,
    hr_after,
    zr_before,
    zr_after,
    pad_f,
    pad_p,
    cells,
    ar_loc,
    ar_mid,
    ar_row,
    ar_col,
    orb,
    g_nb,
    link_h,
    link_l,
    src,
    p_own,
    s_own,
    p_even,
    s_even,
    map_h,
    map_l,
    tmp,
    map_in,
    state_in,
    k_in,
    k_out,
    base,
    greens,
    greens_nb,
    sib_own,
    sib_nb,
    weight,
    send_sem,
    recv_sem,
    local_sem,
):
    n0, n1, n2 = pot.shape
    slabs, n = owner.shape
    slab_cells = n0 // slabs
    assert (nz, slabs) == (8, 4)
    row = min(8, ne)
    cols = ne // row
    e, z = lax.axis_index("energy"), lax.axis_index("slab")
    core = lax.rem(e, 2)
    sibling = (e + 1 - 2 * core, z)
    odd = lax.rem(z, 2) == 1

    def energy(by):
        return (lax.rem(e + (by + ne), ne), z)

    def level(by):
        return (e, lax.rem(z + (by + nz), nz))

    def in_row(k):
        base = (e // row) * row
        return (base + lax.rem(e - base + k, row), z)

    def remote(source, target, index, device):
        return pltpu.make_async_remote_copy(
            src_ref=source,
            dst_ref=target,
            send_sem=send_sem.at[index],
            recv_sem=recv_sem.at[index],
            device_id=device,
            device_id_type=MESH,
        )

    HALO, ROW = 0, 4
    COL = ROW + row - 1
    GEX = COL + cols - 1
    PAIR = GEX + 2 * slabs
    KUP, KDOWN, KBACK = (PAIR + 2 + i * K_PIECES for i in range(3))
    KSIDE = KUP
    AHEAD = KBACK + K_PIECES
    CARRY = AHEAD + 2
    SIB = CARRY + 2
    SIBN = SIB + slabs

    load_small = [
        pltpu.make_async_copy(source, target, local_sem.at[3 + i])
        for i, (source, target) in enumerate(
            ((pot_hbm, pot), (perm_hbm, perm), (charge_hbm, charge), (owner_hbm, owner))
        )
    ]
    for copy in load_small:
        copy.start()
    load_g = pltpu.make_async_copy(g_hbm.at[0], g, local_sem.at[0])
    load_c = pltpu.make_async_copy(cpl_hbm, cpl, local_sem.at[1])
    load_t = pltpu.make_async_copy(tiles_hbm, tiles, local_sem.at[2])
    partners = [in_row(k) for k in range(1, row)] + [energy(row * k) for k in range(1, cols)]
    partners += [energy(by) for by in (1, -1, 2, -2)] + [level(by) for by in (1, -1, 2, -2)]
    barrier = pltpu.get_barrier_semaphore()
    for device in partners:
        pl.semaphore_signal(barrier, inc=1, device_id=device, device_id_type=MESH)

    load_g.start()
    load_c.start()
    load_t.start()
    load_small[0].wait()
    load_small[1].wait()
    for index, ref in enumerate((pot, perm)):
        hs_lo[index] = ref[:, 0:1, :]
        hs_hi[index] = ref[:, n1 - 1 : n1, :]
        zs_lo[index] = ref[0]
        zs_hi[index] = ref[n0 - 1]
    pl.semaphore_wait(barrier, len(partners))

    halos = [
        remote(hs_lo, hr_after, HALO, energy(-1)),
        remote(hs_hi, hr_before, HALO + 1, energy(1)),
        remote(zs_lo, zr_after, HALO + 2, level(-1)),
        remote(zs_hi, zr_before, HALO + 3, level(1)),
    ]
    for copy in halos:
        copy.start()

    load_g.wait()

    def g_copy(s, to_upper):
        side = 0 if to_upper else 1
        return remote(
            g.at[s], g_nb.at[side, s], GEX + side * slabs + s, energy(2 if to_upper else -2)
        )

    load_c.wait()
    EVEN, ODD, BOTH, HALF, FIRST = range(5)

    def keep(high, low, at, parts):
        for k, (h, l) in enumerate(split3(*parts)):
            high[(*at, k)], low[(*at, k)] = h, l

    def link(which, s):
        return [(link_h[which, s, k], link_l[which, s, k]) for k in range(3)]

    def mapping(which):
        return [(map_h[which, k], map_l[which, k]) for k in range(3)]

    def three(ref, *at):
        return split3(ref[(*at, 0)], ref[(*at, 1)])

    def sandwiches(*jobs):
        for slot, (outer, state, _) in enumerate(jobs):
            tmp[slot, 0], tmp[slot, 1] = cprod(state(), outer(), transposed=True)
        for slot, (outer, _, write) in enumerate(jobs):
            write(*cprod(outer(), three(tmp, slot)))

    def added(target, at, *terms):
        def write(real, imag):
            for part, value in enumerate((real, imag)):
                target[(*at, part)] = value + sum(ref[(*where, part)] for ref, where in terms)

        return write

    def make_links(s, *pairs):
        factor = three(cpl, s)
        for which, ref, at in pairs:
            keep(link_h, link_l, (which, s), cprod(three(ref, *at), factor))

    def make_sources(s, *pairs):
        scale = orb[pl.ds(s, 1), :]
        for which, ref, at in pairs:
            real, imag = ref[(*at, 0)], ref[(*at, 1)]
            made = cprod(split3(real * scale, imag * scale), split3(real, imag))
            src[which, s, 0], src[which, s, 1] = real + made[0], imag + made[1]

    @pl.loop(0, slabs)
    def _(s):
        make_links(s, (2, g, (s,)))

    for copy in halos:
        copy.wait()
    for index, (ref, pad) in enumerate(((pot, pad_f), (perm, pad_p))):
        pad[1 : n0 + 1, 1 : n1 + 1, :] = ref[...]
        pad[1 : n0 + 1, 0:1, :] = jnp.where(e > 0, hr_before[index], 0.0)
        pad[1 : n0 + 1, n1 + 1 : n1 + 2, :] = jnp.where(e < ne - 1, hr_after[index], 0.0)
        pad[0, 1 : n1 + 1, :] = jnp.where(z > 0, zr_before[index], 0.0)
        pad[n0 + 1, 1 : n1 + 1, :] = jnp.where(z < nz - 1, zr_after[index], 0.0)
    centre = perm[...]
    field = pot[...]
    lane = lax.broadcasted_iota(jnp.int32, (n0, n1, n2), 2)
    inner0, inner1 = slice(1, n0 + 1), slice(1, n1 + 1)
    windows = [
        (pad_f[2 : n0 + 2, inner1, :], pad_p[2 : n0 + 2, inner1, :]),
        (pad_f[0:n0, inner1, :], pad_p[0:n0, inner1, :]),
        (pad_f[inner0, 2 : n1 + 2, :], pad_p[inner0, 2 : n1 + 2, :]),
        (pad_f[inner0, 0:n1, :], pad_p[inner0, 0:n1, :]),
    ]
    for shift, edge in ((n2 - 1, n2 - 1), (1, 0)):
        windows.append(
            tuple(jnp.where(lane == edge, 0.0, pltpu.roll(x, shift, 2)) for x in (field, centre))
        )
    load_small[2].wait()
    load_small[3].wait()
    numerator = charge[...]
    denominator = jnp.zeros_like(numerator)
    for near_field, near_perm in windows:
        face = 0.5 * (centre + near_perm)
        numerator = numerator + face * near_field
        denominator = denominator + face
    swept = numerator / denominator
    pot_out[...] = swept
    for plane in range(n0):
        cells[pl.ds(plane * n1, n1), :] = swept[plane]

    depth_bits = int(math.log2(n2))
    cross_bits = int(math.log2(n1 * ne))
    rows = slab_cells * n1
    for s in range(slabs):
        index = owner[s : s + 1, :]
        first = index >> (depth_bits + cross_bits)
        second = ((index >> depth_bits) & (n1 * ne - 1)) - e * n1
        third = index & (n2 - 1)
        chosen = jnp.where(
            lax.broadcasted_iota(jnp.int32, (n2, n), 0) == third, 1.0, 0.0
        ).astype(BF16)
        block = cells[pl.ds(s * rows, rows), :]
        high, low = split(block)
        lowest = (block - high.astype(F32) - low.astype(F32)).astype(BF16)
        picked = sum(
            jnp.dot(piece, chosen, preferred_element_type=F32) for piece in (high, low, lowest)
        )
        here = (second >= 0) & (second < n1)
        at = jnp.where(here, first * n1 + second, -1)
        mine = lax.broadcasted_iota(jnp.int32, (rows, n), 0) == at
        ar_loc[s : s + 1, :] = jnp.sum(jnp.where(mine, picked, 0.0), axis=0, keepdims=True)

    row_copies = [remote(ar_loc, ar_row.at[k - 1], ROW + k - 1, in_row(k)) for k in range(1, row)]
    for copy in row_copies:
        copy.start()

    tmp[0, 0], tmp[0, 1] = cprod(link(2, 1), link(2, 0))
    keep(map_h, map_l, (HALF,), cprod(link(2, 3), link(2, 2)))
    p_own[0], p_own[1] = cprod(mapping(HALF), three(tmp, 0))

    send_p = remote(p_own, p_even, PAIR, level(1))

    @pl.when(jnp.logical_and(jnp.logical_not(odd), z > 0))
    def _():
        send_p.start()

    for copy in row_copies:
        copy.wait()
    total = ar_loc[...]
    for k in range(1, row):
        total = total + ar_row[k - 1]
    ar_mid[...] = total
    col_copies = [
        remote(ar_mid, ar_col.at[k - 1], COL + k - 1, energy(row * k)) for k in range(1, cols)
    ]
    for copy in col_copies:
        copy.start()
    for copy in col_copies:
        copy.wait()
    total = ar_mid[...]
    for k in range(1, cols):
        total = total + ar_col[k - 1]
    orb[...] = total

    for s in range(1, slabs):
        g_copy(s, True).start()
        g_copy(s, False).start()

    @pl.loop(0, slabs)
    def _(s):
        make_sources(s, (2, g, (s,)))

    sandwiches(
        (lambda: link(2, 1), lambda: three(src, 2, 0), added(base, (), (src, (2, 1)))),
        (lambda: link(2, 3), lambda: three(src, 2, 2), added(k_out, (), (src, (2, 3)))),
    )
    sandwiches((lambda: mapping(HALF), lambda: three(base), added(s_own, (), (k_out, ()))))

    send_s = remote(s_own, s_even, PAIR + 1, level(1))

    @pl.when(jnp.logical_not(odd))
    def _():
        send_s.start()

    def make_weights():
        load_t.wait()
        for offset in (1, 2):
            raise_now = jnp.zeros((n, n), F32)
            lower_now = jnp.zeros((n, n), F32)
            for mode in range(tiles.shape[0]):
                hit = jnp.where(shifts[mode] == offset, 1.0, 0.0)
                raise_now = raise_now + (hit * occ[mode]) * tiles[mode]
                lower_now = lower_now + (hit * (occ[mode] + 1.0)) * tiles[mode]
            raise_now = jnp.where(e + offset < ne, raise_now, 0.0)
            lower_now = jnp.where(e >= offset, lower_now, 0.0)
            if offset == 2:
                weight[0], weight[1] = lower_now, raise_now
            else:
                weight[2] = jnp.where(core == 0, raise_now, lower_now)
                weight[3] = jnp.where(core == 0, lower_now, raise_now)

    def prepare_neighbours(first, last):
        def one(s, nothing):
            for side in range(2):
                g_copy(s, side == 0).wait_recv()
            both = [(side, g_nb, (side, s)) for side in range(2)]
            make_links(s, *both)
            make_sources(s, *both)

            @pl.when(s > 1)
            def _():
                sandwiches(
                    *(
                        (
                            lambda side=side: link(side, s),
                            lambda side=side: three(src, side, s - 1),
                            added(src, (side, s), (src, (side, s))),
                        )
                        for side in range(2)
                    )
                )
                for side in range(2):
                    keep(link_h, link_l, (side, s), cprod(link(side, s), link(side, s - 1)))

            return nothing

        lax.fori_loop(first, last, one, 0)

    make_weights()

    def k_slices():
        rows_each = n // (K_PIECES // 2)
        return [
            (part, pl.ds(h * rows_each, rows_each))
            for h in range(K_PIECES // 2)
            for part in range(2)
        ]

    def k_piece(source, first, i, device):
        at = k_slices()[i]
        return remote(source.at[at], k_in.at[at], first + i, device)

    pieces = range(K_PIECES)
    k_up = [k_piece(k_out, KUP, i, level(2)) for i in pieces]
    k_down = [k_piece(k_in, KDOWN, i, level(-1)) for i in pieces]
    k_side = [k_piece(k_in, KSIDE, i, level(1)) for i in pieces]
    through_ring = range(K_AHEAD, K_PIECES)
    k_back = {i: k_piece(k_out, KBACK, i, level(-2)) for i in through_ring}
    k_relay = {i: k_piece(k_in, KBACK, i, level(-2)) for i in through_ring}
    ahead = [
        remote(p_even, map_in, AHEAD, level(1)),
        remote(s_own, state_in, AHEAD + 1, level(1)),
    ]
    ahead_relay = [
        remote(map_in, map_in, AHEAD, level(1)),
        remote(state_in, state_in, AHEAD + 1, level(1)),
    ]

    def pair_state():
        keep(map_h, map_l, (ODD,), (p_own[0], p_own[1]))
        send_s.wait_recv()
        sandwiches((lambda: mapping(ODD), lambda: three(s_even), added(s_own, (), (s_own, ()))))

    def pair_maps():
        send_p.wait_recv()
        keep(map_h, map_l, (EVEN,), (p_even[0], p_even[1]))

    def own_green(s, outer, ref, at, term):
        sandwiches((outer, lambda: three(ref, *at), added(greens, (s,), term)))

    def map_through(which):
        keep(map_h, map_l, (FIRST,), cprod(link(2, 0), mapping(which)))

    def add_through(state):
        sandwiches(
            (lambda: link(2, 0), lambda: three(state), added(base, (), (src, (2, 0))))
        )

    def first_green():
        own_green(0, lambda: mapping(FIRST), k_in, (), (base, ()))

    def receive_and_hand_on(copies, *onward, these=pieces):
        for i in these:
            copies[i].wait_recv()
            for copy in onward:
                copy[i].start()

    early = jnp.where(z >= 6, slabs - 1, jnp.where(odd, 1, slabs))

    @pl.when(z == 0)
    def _():
        greens[0] = src[2, 0]

    @pl.when(z == 1)
    def _():
        pair_state()
        k_out[...] = s_own[...]
        for copy in k_up:
            copy.start()
        own_green(0, lambda: link(2, 0), s_even, (), (src, (2, 0)))

    @pl.when(jnp.logical_or(z == 3, z == 5))
    def _():
        pair_maps()
        keep(map_h, map_l, (ODD,), (p_own[0], p_own[1]))
        both = cprod(mapping(ODD), mapping(EVEN))

        @pl.when(z == 3)
        def _():
            keep(map_h, map_l, (BOTH,), both)

        @pl.when(z == 5)
        def _():
            p_even[0], p_even[1] = both
            ahead[0].start()

        pair_state()

        @pl.when(z == 5)
        def _():
            ahead[1].start()

        map_through(EVEN)
        add_through(s_even)

    @pl.when(z == 7)
    def _():
        pair_maps()
        send_s.wait_recv()
        ahead[0].wait_recv()
        keep(map_h, map_l, (BOTH,), cprod(mapping(EVEN), three(map_in)))
        map_through(BOTH)

    @pl.when(z == 6)
    def _():
        for copy, relay in zip(ahead, ahead_relay):
            copy.wait_recv()
            relay.start()
        keep(map_h, map_l, (BOTH,), (map_in[0], map_in[1]))
        map_through(BOTH)
        add_through(state_in)

    prepare_neighbours(1, early)

    @pl.when(z == 3)
    def _():
        receive_and_hand_on(k_up, k_down)
        sandwiches((lambda: mapping(BOTH), lambda: three(k_in), added(k_out, (), (s_own, ()))))
        for i in through_ring:
            k_back[i].start()
        for i in pieces:
            k_up[i].start()

    @pl.when(z == 5)
    def _():
        receive_and_hand_on(k_up, k_side, k_down)

    @pl.when(jnp.logical_or(z == 3, z == 5))
    def _():
        first_green()

    @pl.when(z == 7)
    def _():
        ahead[1].wait_recv()
        sandwiches(
            (lambda: mapping(EVEN), lambda: three(state_in), added(k_out, (), (s_even, ())))
        )
        add_through(k_out)
        receive_and_hand_on(k_side, these=range(K_AHEAD))
        receive_and_hand_on(k_back, these=through_ring)
        first_green()

    @pl.when(jnp.logical_or(z == 2, z == 4))
    def _():
        receive_and_hand_on(k_down)
        own_green(0, lambda: link(2, 0), k_in, (), (src, (2, 0)))

    @pl.when(z == 6)
    def _():
        receive_and_hand_on(k_side, k_side, these=range(K_AHEAD))
        receive_and_hand_on(k_side, these=through_ring)
        first_green()

    def first_copy(side):
        return remote(
            greens.at[0],
            greens_nb.at[side, 0],
            CARRY + side,
            energy(2 if side == 0 else -2),
        )

    def own_copy(s):
        return remote(greens.at[s], sib_own.at[s], SIB + s, sibling)

    for side in range(2):
        first_copy(side).start()
    own_copy(0).start()

    @pl.loop(1, slabs)
    def _(s):
        own_green(s, lambda: link(2, s), greens, (s - 1,), (src, (2, s)))
        own_copy(s).start()

    @pl.when(z == 1)
    def _():
        receive_and_hand_on(k_back, k_relay, these=through_ring)

    prepare_neighbours(early, slabs)

    def far_copy(side, s):
        return remote(greens_nb.at[side, s], sib_nb.at[s], SIBN + s, sibling)

    def far_greens(side, use):
        def write(s):
            return lambda *made: use(s, *(made[part] + src[side, s, part] for part in range(2)))

        sandwiches(
            *(
                (lambda s=s: link(side, s), lambda: three(greens_nb, side, 0), write(s))
                for s in range(1, slabs)
            )
        )

    def mix_most(s, part, near):
        se_out[0, s, part] = (
            weight[core] * near
            + weight[1 - core] * greens_nb[1 - core, s, part]
            + weight[2] * sib_own[s, part]
        )

    for side in range(2):
        first_copy(side).wait_recv()
    far_copy(1 - core, 0).start()

    def store_and_send(s, real, imag):
        greens_nb[1 - core, s, 0], greens_nb[1 - core, s, 1] = real, imag
        far_copy(1 - core, s).start()

    def mix_both(s, real, imag):
        mix_most(s, 0, real)
        mix_most(s, 1, imag)

    far_greens(1 - core, store_and_send)
    for s in range(slabs):
        own_copy(s).wait_recv()
    mix_both(0, greens_nb[core, 0, 0], greens_nb[core, 0, 1])
    far_greens(core, mix_both)

    @pl.loop(0, slabs)
    def _(s):
        far_copy(0, s).wait_recv()
        for part in range(2):
            se_out[0, s, part] = se_out[0, s, part] + weight[3] * sib_nb[s, part]

    for s in range(slabs):
        own_copy(s).wait_send()
        far_copy(0, s).wait_send()
    for s in range(1, slabs):
        g_copy(s, True).wait_send()
        g_copy(s, False).wait_send()
    for side in range(2):
        first_copy(side).wait_send()

    def sent(condition, *copies):
        @pl.when(condition)
        def _():
            for copy in copies:
                copy.wait_send()

    sent(jnp.logical_not(odd), send_s)
    sent(jnp.logical_and(jnp.logical_not(odd), z > 0), send_p)
    sent(jnp.logical_or(z == 1, z == 3), *k_up)
    sent(jnp.logical_or(z == 3, z == 5), *k_down)
    sent(z == 5, *k_side)
    sent(z == 6, *k_side[:K_AHEAD])
    sent(z == 3, *k_back.values())
    sent(z == 1, *k_relay.values())
    sent(z == 5, *ahead)
    sent(z == 6, *ahead_relay)


def per_device(
    ne,
    nz,
    potential_old,
    charge,
    permittivity,
    owner_cell,
    green_free,
    coupling,
    shifts,
    occupation,
    mode_tiles,
):
    n0, n1, n2 = potential_old.shape
    slabs, n = owner_cell.shape
    modes = mode_tiles.shape[0]
    vmem = pl.BlockSpec(memory_space=pltpu.VMEM)
    smem = pl.BlockSpec(memory_space=pltpu.SMEM)
    hbm = pl.BlockSpec(memory_space=pl.ANY)
    row = min(8, ne)
    cols = ne // row
    block = (2, n, n)
    sems = 4 + row - 1 + cols - 1 + 2 * slabs + 2 + 3 * K_PIECES + 2 + 2 + 2 * slabs
    scratch = [
        pltpu.VMEM((n0, n1, n2), F32),
        pltpu.VMEM((n0, n1, n2), F32),
        pltpu.VMEM((n0, n1, n2), F32),
        pltpu.VMEM((slabs, n), jnp.int32),
        pltpu.VMEM((slabs,) + block, F32),
        pltpu.VMEM((slabs,) + block, F32),
        pltpu.VMEM((modes, n, n), F32),
        pltpu.VMEM((2, n0, 1, n2), F32),
        pltpu.VMEM((2, n0, 1, n2), F32),
        pltpu.VMEM((2, n1, n2), F32),
        pltpu.VMEM((2, n1, n2), F32),
        pltpu.VMEM((2, n0, 1, n2), F32),
        pltpu.VMEM((2, n0, 1, n2), F32),
        pltpu.VMEM((2, n1, n2), F32),
        pltpu.VMEM((2, n1, n2), F32),
        pltpu.VMEM((n0 + 2, 8, n2), F32),
        pltpu.VMEM((n0 + 2, 8, n2), F32),
        pltpu.VMEM((n0 * n1, n2), F32),
        pltpu.VMEM((slabs, n), F32),
        pltpu.VMEM((slabs, n), F32),
        pltpu.VMEM((row, slabs, n), F32),
        pltpu.VMEM((cols, slabs, n), F32),
        pltpu.VMEM((slabs, n), F32),
        pltpu.VMEM((2, slabs) + block, F32),
        pltpu.VMEM((3, slabs, 3, n, n), BF16),
        pltpu.VMEM((3, slabs, 3, n, n), BF16),
        pltpu.VMEM((3, slabs) + block, F32),
        pltpu.VMEM(block, F32),
        pltpu.VMEM(block, F32),
        pltpu.VMEM(block, F32),
        pltpu.VMEM(block, F32),
        pltpu.VMEM((5, 3, n, n), BF16),
        pltpu.VMEM((5, 3, n, n), BF16),
        pltpu.VMEM((3,) + block, F32),
        pltpu.VMEM(block, F32),
        pltpu.VMEM(block, F32),
        pltpu.VMEM(block, F32),
        pltpu.VMEM(block, F32),
        pltpu.VMEM(block, F32),
        pltpu.VMEM((slabs,) + block, F32),
        pltpu.VMEM((2, slabs) + block, F32),
        pltpu.VMEM((slabs,) + block, F32),
        pltpu.VMEM((slabs,) + block, F32),
        pltpu.VMEM((4, n, n), F32),
        pltpu.SemaphoreType.DMA((sems,)),
        pltpu.SemaphoreType.DMA((sems,)),
        pltpu.SemaphoreType.DMA((7,)),
    ]
    return pl.pallas_call(
        functools.partial(kernel, ne, nz),
        out_shape=(
            pltpu.VMEM((n0, n1, n2), F32),
            pltpu.VMEM((1, slabs) + block, F32),
        ),
        in_specs=[hbm, hbm, hbm, hbm, hbm, hbm, smem, smem, hbm],
        out_specs=(vmem, vmem),
        scratch_shapes=scratch,
        compiler_params=pltpu.CompilerParams(
            collective_id=0, has_side_effects=True, vmem_limit_bytes=54 << 20
        ),
    )(
        potential_old,
        charge,
        permittivity,
        owner_cell,
        green_free,
        coupling,
        shifts,
        occupation,
        mode_tiles,
    )


def solution(mesh):
    in_specs = (
        P("slab", "energy", None),
        P("slab", "energy", None),
        P("slab", "energy", None),
        P("slab", None),
        P("energy", "slab", None, None, None),
        P("slab", None, None, None),
        P(),
        P(),
        P(),
    )
    out_specs = (P("slab", "energy", None), P("energy", "slab", None, None, None))
    return jax.shard_map(
        functools.partial(per_device, mesh.shape["energy"], mesh.shape["slab"]),
        mesh=mesh,
        in_specs=in_specs,
        out_specs=out_specs,
        check_vma=False,
    )
```
